256 devices in a mesh: seq: 16 (over z_lo, x), dp: 4 (over y), tp: 4 (over z_hi, core).
Axes of the slice: x: 4, y: 4, z: 8 (z_hi: 2, z_lo: 4; z = z_hi * 4 + z_lo), core: 2. Of those that a mesh axis runs over, the one named last changes fastest.
Arguments:
- patches: bfloat16 [16, 3072, 1152], P(('dp', 'tp'), 'seq'), parts along dimension 0, may hold values from -6 to 6
- seg_ids: int32 [16, 3072], P(('dp', 'tp'), 'seq'), parts along dimension 0, may hold values from 0 to 11, never falling along the last dimension, each value on 1 to 768 neighbouring positions
- pos_rows: int32 [16, 3072], P(('dp', 'tp'), 'seq'), parts along dimension 0, may hold values from 0 to 63
- pos_cols: int32 [16, 3072], P(('dp', 'tp'), 'seq'), parts along dimension 0, may hold values from 0 to 63
- row_table: bfloat16 [64, 1152], replicated, may hold values from -3 to 3
- col_table: bfloat16 [64, 1152], replicated, may hold values from -3 to 3
- ln1_gain: float32 [1152], replicated, may hold values from 0.5 to 1.5
- ln1_bias: float32 [1152], replicated, may hold values from -1.75 to 1.75
- w_qkv: bfloat16 [1152, 3456], P(None, 'seq'), may hold values from -0.41247896 to 0.41247896
- w_out: bfloat16 [1152, 1152], P('seq'), may hold values from -0.1875 to 0.1875
- out_bias: bfloat16 [1152], replicated, may hold values from -3 to 3
- ln2_gain: float32 [1152], replicated, may hold values from 0.5 to 1.5
- ln2_bias: float32 [1152], replicated, may hold values from -1.75 to 1.75
- w_fc1: bfloat16 [1152, 4304], P(None, 'tp'), may hold values from -0.1875 to 0.1875
- fc1_bias: bfloat16 [4304], P('tp'), may hold values from -3 to 3
- w_fc2: bfloat16 [4304, 1152], P('tp'), may hold values from -0.09375 to 0.09375
- fc2_bias: bfloat16 [1152], replicated, may hold values from -3 to 3
Outputs:
- encoded: bfloat16 [16, 3072, 1152], P(('dp', 'tp'), 'seq'), parts along dimension 0
The draws below stay inside these ranges and needn't reach their ends.
There are 4 independent parts, one for each index of `dp`. The reference program is written for one: setup_inputs(seed, part) draws one part's arguments, and reference() takes and returns one part's arrays. A program takes and returns all parts, laid end to end along the dimension named above; an argument that names none is the same for every part. Nothing has to cross between parts.
Inputs may be any that keep to these rules, and one draw needn't show every extreme that they name: `seg_ids`: image numbers never fall along a sequence; every image has 1 to 768 tokens.
All inputs are finite; a program needn't handle non-finite values.
Results may differ from the reference program's by a relative error of at most 0.0095.
Values may be sent and summed in bfloat16 or wider, within the bound.
A program may use at most 64 MiB of HBM per device.

```python
import math
import jax
import jax.numpy as jnp
import numpy as np
from jax import lax

D = 1152
HEADS = 16
FF = 4304
GRID = 64
IMAGES = 12
HEAD_DIM = 72
LENGTH = 3072
NSEQ = 4
MOST = 768


def draw_w_qkv(key, part):
    head_dim = D // HEADS
    shape = (D, HEADS, 3, head_dim)
    weights = jnp.clip(jax.random.normal(key, shape, jnp.float32), -6.0, 6.0) / jnp.sqrt(float(D))
    return weights.reshape(D, HEADS * 3 * head_dim).astype(jnp.bfloat16)


def touch_ends(result, rng, smallest, top_value):
    longest = result.shape.index(max(result.shape))
    spots = []
    for shift in (0, 1):
        where = [jax.random.randint(jax.random.fold_in(rng, axis), (), 0, length) for axis, length in enumerate(result.shape)]
        where[longest] = (where[longest] + shift) % result.shape[longest]
        spots.append(tuple(where))
    return result.at[spots[0]].set(smallest).at[spots[1]].set(top_value)


def steps_of(rng, shape, shards, least, top_value):
    level = 1.0
    for dim, blocks in shards:
        heights = jax.random.uniform(jax.random.fold_in(jax.random.fold_in(rng, 6), dim), (blocks,), jnp.float32, least / len(shards), top_value / len(shards))
        level = level * jnp.repeat(jnp.exp(heights), shape[dim] // blocks).reshape((-1,) + (1,) * (len(shape) - 1 - dim))
    return level


def length_profile(number_of, total, reach, slope):
    weights = [(1 << 20) // math.isqrt(standing ** slope) + 1 for standing in range(2, number_of + 1)]
    surplus, holding = total - reach - (number_of - 1), [1] * (number_of - 1)
    while surplus > 0:
        movable = [i for i in range(number_of - 1) if holding[i] < reach]
        mass, budget = sum([weights[i] for i in movable]), surplus
        for i in movable:
            addition = min(reach - holding[i], max(1, budget * weights[i] // mass), surplus)
            holding[i] = holding[i] + addition
            surplus = surplus - addition
    return np.array([reach] + holding)


def ragged(own_key, number_of, total, most, lean):
    if number_of == 2:
        one = jax.random.randint(own_key, (), max(1, total - most), min(most, total - 1) + 1)
        return jnp.stack([one, total - one])
    tallies = jnp.asarray(length_profile(number_of, total, most, lean), jnp.int32)
    couples = (number_of - 1) // 2
    donor, taker = tallies[1:1 + 2 * couples:2], tallies[2:2 + 2 * couples:2]
    slack = jnp.minimum(donor - 1, most - taker)
    shifted = jax.random.randint(jax.random.fold_in(own_key, 1), (couples,), 0, 1 << 20) % (slack + 1)
    tallies = tallies.at[1:1 + 2 * couples:2].set(donor - shifted).at[2:2 + 2 * couples:2].set(taker + shifted)
    return tallies[jax.random.permutation(jax.random.fold_in(own_key, 2), number_of)]


def scatter_about(key, dims, scale, most, pieces=(), dtype=jnp.bfloat16):
    factor_of = steps_of(key, dims, pieces, -0.22, 0.18) if pieces else 1.0
    drawn = jax.random.normal(key, dims, jnp.float32) * scale * factor_of
    return jnp.minimum(jnp.maximum(drawn, -most), most).astype(dtype)


def setup_inputs(seed: int = 0, part: int = 0) -> dict:
    seeds = jax.random.split(jax.random.key(seed), 18)
    part_keys = jax.random.split(jax.random.fold_in(seeds[17], part), 18)
    return {
        "patches": scatter_about(part_keys[0], (NSEQ, LENGTH, D), 1.0, 6.0, ((0, 4), (1, 16))),
        "seg_ids": jax.vmap(lambda own: jnp.searchsorted(jnp.cumsum(ragged(own, IMAGES, LENGTH, MOST, 1)), jnp.arange(LENGTH), side="right"))(jax.random.split(part_keys[1], NSEQ)).reshape((NSEQ, LENGTH)).astype(jnp.int32),
        "pos_rows": touch_ends(jax.random.randint(part_keys[2], (NSEQ, LENGTH), 0, GRID), jax.random.fold_in(part_keys[2], 1), 0, GRID - 1).astype(jnp.int32),
        "pos_cols": touch_ends(jax.random.randint(part_keys[3], (NSEQ, LENGTH), 0, GRID), jax.random.fold_in(part_keys[3], 1), 0, GRID - 1).astype(jnp.int32),
        "row_table": scatter_about(seeds[4], (GRID, D), 0.5, 3.0),
        "col_table": scatter_about(seeds[5], (GRID, D), 0.5, 3.0),
        "ln1_gain": jnp.clip(1.0 + 0.1 * jax.random.normal(seeds[6], (D,), jnp.float32), 0.5, 1.5),
        "ln1_bias": scatter_about(seeds[7], (D,), 0.3, 1.75, (), jnp.float32),
        "w_qkv": draw_w_qkv(jax.random.fold_in(seeds[17], 71), part),
        "w_out": scatter_about(seeds[9], (D, D), D ** -0.5, 0.1875, ((0, 16),)),
        "out_bias": scatter_about(seeds[10], (D,), 0.5, 3.0),
        "ln2_gain": jnp.clip(1.0 + 0.1 * jax.random.normal(seeds[11], (D,), jnp.float32), 0.5, 1.5),
        "ln2_bias": scatter_about(seeds[12], (D,), 0.3, 1.75, (), jnp.float32),
        "w_fc1": scatter_about(seeds[13], (D, FF), D ** -0.5, 0.1875, ((1, 4),)),
        "fc1_bias": scatter_about(seeds[14], (FF,), 0.5, 3.0, ((0, 4),)),
        "w_fc2": scatter_about(seeds[15], (FF, D), FF ** -0.5, 0.09375, ((0, 4),)),
        "fc2_bias": scatter_about(seeds[16], (D,), 0.5, 3.0),
    }


def layer_norm(values, gain, shift):
    center = lax.optimization_barrier(jnp.mean(values, -1, keepdims=True))
    spread = lax.optimization_barrier(jnp.mean(jnp.square(values - center), -1, keepdims=True))
    return (values - center) * lax.rsqrt(spread + 1e-06) * gain + shift

def attend_one(item, segments):
    query = item[:, 0]
    keys = item[:, 1]
    value = item[:, 2]
    scores = jnp.dot(query, keys.T, preferred_element_type=jnp.float32) / math.sqrt(query.shape[-1])
    same = segments[:, None] == segments[None, :]
    scores = jnp.where(same, scores, -jnp.inf)
    top = lax.optimization_barrier(jnp.max(scores, -1, keepdims=True))
    expo = jnp.exp(scores - top)
    probs = (expo / lax.optimization_barrier(jnp.sum(expo, -1, keepdims=True))).astype(jnp.bfloat16)
    return jnp.dot(probs, value, preferred_element_type=jnp.float32).astype(jnp.bfloat16)

def reference(patches, seg_ids, pos_rows, pos_cols, row_table, col_table, ln1_gain, ln1_bias, w_qkv, w_out, out_bias, ln2_gain, ln2_bias, w_fc1, fc1_bias, w_fc2, fc2_bias):
    embedded = patches.astype(jnp.float32) + row_table[pos_rows].astype(jnp.float32) + col_table[pos_cols].astype(jnp.float32)
    embedded = embedded.reshape(NSEQ * LENGTH, D)
    normed = layer_norm(embedded, ln1_gain, ln1_bias).astype(jnp.bfloat16)
    qkv = jnp.dot(normed, w_qkv, preferred_element_type=jnp.float32).astype(jnp.bfloat16)
    qkv = qkv.reshape(NSEQ, LENGTH, HEADS, 3, HEAD_DIM).transpose(0, 2, 1, 3, 4)
    qkv = qkv.reshape(NSEQ * HEADS, LENGTH, 3, HEAD_DIM)
    segments = jnp.repeat(seg_ids, HEADS, axis=0)
    mixed = lax.map(lambda pair: attend_one(pair[0], pair[1]), (qkv, segments))
    mixed = mixed.reshape(NSEQ, HEADS, LENGTH, HEAD_DIM).transpose(0, 2, 1, 3).reshape(NSEQ * LENGTH, D)
    attended = embedded + jnp.dot(mixed, w_out, preferred_element_type=jnp.float32) + out_bias.astype(jnp.float32)
    normed2 = layer_norm(attended, ln2_gain, ln2_bias).astype(jnp.bfloat16)
    hidden = jax.nn.gelu(jnp.dot(normed2, w_fc1, preferred_element_type=jnp.float32) + fc1_bias.astype(jnp.float32), approximate=True).astype(jnp.bfloat16)
    reduced = jnp.dot(hidden, w_fc2, preferred_element_type=jnp.float32)
    encoded = (attended + reduced + fc2_bias.astype(jnp.float32)).astype(jnp.bfloat16)
    return encoded.reshape(NSEQ, LENGTH, D)
```

```python
import math

import jax
import jax.numpy as jnp
from jax import lax
from jax.experimental import pallas as pl
from jax.experimental.pallas import tpu as pltpu
from jax.sharding import Mesh
from jax.sharding import PartitionSpec as P

AXES = ("zl", "x", "y", "zh", "c")
SEQ = ("zl", "x")
BATCH = ("y", "zh", "c")
MESH_ID = pl.DeviceIdType.MESH
TOK = 192
WIDTH = 1152
ROW = 4 * TOK
HEAD = 72
WINDOW = 9 * TOK
QROWS = 224
OROWS = 96
F32 = jnp.float32
BF16 = jnp.bfloat16
NT = (((1,), (1,)), ((), ()))


def norm_rows(values, gain, shift):
    center = jnp.mean(values, -1, keepdims=True)
    moved = values - center
    spread = jnp.mean(jnp.square(moved), -1, keepdims=True)
    return moved * lax.rsqrt(spread + 1e-06) * gain + shift


def gelu(u):
    return 0.5 * u * (1.0 + jnp.tanh(math.sqrt(2.0 / math.pi) * (u + 0.044715 * u * u * u)))


def layer_kernel(
    patches,
    ints,
    rows_tab,
    cols_tab,
    vecs,
    w_a,
    w_b,
    w_f,
    out,
    emb,
    nrm,
    segs,
    seg_keys,
    seg_query,
    wz,
    wb,
    wp,
    wo,
    qs,
    kv,
    part_out,
    part_in,
    own_part,
    f_own,
    f_far,
    vecs_far,
    n2,
    hid,
    mlp,
    mlp_out,
    mlp_in,
    loc_sem,
    a_send,
    a_recv,
    as_send,
    as_recv,
    b_send,
    b_recv,
    bs_send,
    bs_recv,
    n_send,
    n_recv,
    s_send,
    s_recv,
    k_send,
    k_recv,
    f_send,
    f_recv,
    fx_send,
    fx_recv,
    fy_send,
    fy_recv,
    r_send,
    r_recv,
    m_send,
    m_recv,
):
    zl, x, y, zh, c = (lax.axis_index(a) for a in AXES)
    z = zh * 4 + zl

    def device(dz=0, dx=0, dy=0, dc=0, mirror=False):
        zz = 7 - z if mirror else lax.rem(z + dz + 8, 8)
        return {
            "zl": lax.rem(zz, 4),
            "x": lax.rem(x + dx + 4, 4),
            "y": lax.rem(y + dy + 4, 4),
            "zh": zz // 4,
            "c": lax.rem(c + dc, 2),
        }

    def remote(src, dst, send, recv, **where):
        return pltpu.make_async_remote_copy(
            src_ref=src,
            dst_ref=dst,
            send_sem=send,
            recv_sem=recv,
            device_id=device(**where),
            device_id_type=MESH_ID,
        )

    def around(v, d):
        return lax.rem(v + d + 4, 4)

    has_prev = zl > 0
    has_next = zl < 3

    barrier = pltpu.get_barrier_semaphore()
    peers = (
        [dict(dz=d) for d in (1, -1, 2, -2)]
        + [dict(dx=d) for d in (1, -1, 2)]
        + [dict(dy=d) for d in (1, -1, 2)]
        + [dict(dc=1), dict(mirror=True)]
    )
    for peer in peers:
        pl.semaphore_signal(barrier, inc=1, device_id=device(**peer), device_id_type=MESH_ID)
    pl.semaphore_wait(barrier, len(peers))

    local_a = pltpu.make_async_copy(w_a, wz.at[zl], loc_sem.at[0])
    local_b = pltpu.make_async_copy(w_b, wb.at[zl], loc_sem.at[1])
    local_f = pltpu.make_async_copy(w_f, f_own, loc_sem.at[2])
    local_a.start()

    def slab(src, dst, first, rows, send, recv, k, dz):
        at = pl.ds(pl.multiple_of(first, 16), rows)
        return remote(src.at[at], dst.at[zl, at], send.at[k], recv.at[k], dz=dz)

    half_a = c * (QROWS // 2)
    copies_a = [
        slab(w_a, wz, half_a, 112, a_send, a_recv, 0, 1),
        slab(w_a, wz, half_a, 112, a_send, a_recv, 1, -1),
        slab(w_a, wz, half_a, 64, a_send, a_recv, 2, 2),
        slab(w_a, wz, half_a + 64, 48, a_send, a_recv, 3, -2),
    ]
    for copy in copies_a:
        copy.start()
    local_b.start()
    local_f.start()

    ints_f = ints[...].astype(F32)
    level = lax.broadcasted_iota(jnp.int32, (128, 256), 0).astype(F32)
    wanted = jnp.where(level < 64.0, ints_f[1:2, :], ints_f[2:3, :] + 64.0)
    hot = jnp.transpose(jnp.where(level == wanted, 1.0, 0.0))[:TOK].astype(BF16)
    tables = jnp.concatenate([rows_tab[...], cols_tab[...]], axis=0)
    embedded = patches[...].astype(F32) + jnp.dot(hot, tables, preferred_element_type=F32)
    emb[...] = embedded
    nrm[x] = norm_rows(embedded, vecs[0:1, :], vecs[1:2, :]).astype(BF16)
    segs[1, x] = jnp.broadcast_to(ints_f[0:1, :], (8, 256))

    copies_n = []
    copies_s = []
    for k, dx in enumerate((1, -1, 2)):
        copies_n.append(remote(nrm.at[x], nrm.at[x], n_send.at[k], n_recv.at[k], dx=dx))
        copies_s.append(
            remote(segs.at[1, x], segs.at[1, x], s_send.at[k], s_recv.at[k], dx=dx)
        )
    for copy in copies_s + copies_n:
        copy.start()

    wp[...] = jnp.zeros_like(wp)
    wo[...] = jnp.zeros_like(wo)

    @pl.when(jnp.logical_not(has_prev))
    def _():
        kv[0:ROW, :] = jnp.zeros((ROW, 640), BF16)
        segs[0] = jnp.full((4, 8, 256), -1.0, F32)

    @pl.when(jnp.logical_not(has_next))
    def _():
        kv[2 * ROW : 3 * ROW, :] = jnp.zeros((ROW, 640), BF16)
        segs[2] = jnp.full((4, 8, 256), -1.0, F32)

    def to_sibling(buf, first, rows, send, recv):
        at = pl.ds(pl.multiple_of(first, 16), rows)
        made = []
        for k, d in enumerate((-1, 1, 2)):
            ref = buf.at[around(zl, d), at]
            made.append(remote(ref, ref, send.at[k], recv.at[k], dc=1))
        return made

    copies_as = to_sibling(wz, half_a, QROWS // 2, as_send, as_recv)
    for copy in copies_a:
        copy.wait_recv()
    for copy in copies_as:
        copy.start()

    def piece(px):
        return pl.ds(pl.multiple_of((y * 4 + px) * 144, 16), 144)

    cross = remote(w_f.at[piece(x)], f_far.at[piece(x)], f_send.at[0], f_recv.at[0], mirror=True)
    cross_v = remote(vecs, vecs_far, f_send.at[1], f_recv.at[1], mirror=True)
    cross.start()
    cross_v.start()

    local_a.wait()
    for copy in copies_as:
        copy.wait_recv()
    for h in range(4):
        wp[144 * h : 144 * h + 80, :] = wz[h, 0:80, :]
        wp[512 + 144 * h : 656 + 144 * h, :] = wz[h, 80:QROWS, :]

    copies_k = []

    def project(k, source):
        tokens = nrm[source]
        at = pl.ds(pl.multiple_of(source * TOK, TOK), TOK)
        qs[at, :] = lax.dot_general(
            tokens, wp[0:512, :], NT, preferred_element_type=F32
        ).astype(BF16)
        here = pl.ds(pl.multiple_of(ROW + source * TOK, TOK), TOK)
        kv[here, :] = lax.dot_general(
            tokens, wp[512:1152, :], NT, preferred_element_type=F32
        ).astype(BF16)
        as_next = pl.ds(pl.multiple_of(2 * ROW + source * TOK, TOK), TOK)
        up = remote(kv.at[here], kv.at[at], k_send.at[0, k], k_recv.at[0, k], dz=1)
        down = remote(kv.at[here], kv.at[as_next], k_send.at[1, k], k_recv.at[1, k], dz=-1)
        copies_k.append((up, down))
        pl.when(has_next)(up.start)
        pl.when(has_prev)(down.start)

    project(0, x)
    for k, dx in enumerate((-1, 1, 2)):
        copies_n[k].wait_recv()
        project(k + 1, around(x, dx))
    for copy in copies_s:
        copy.wait_recv()
    seg_up = remote(segs.at[1], segs.at[0], s_send.at[3], s_recv.at[3], dz=1)
    seg_down = remote(segs.at[1], segs.at[2], s_send.at[4], s_recv.at[4], dz=-1)
    pl.when(has_next)(seg_up.start)
    pl.when(has_prev)(seg_down.start)

    half_b = c * (OROWS // 2)
    copies_b = [
        slab(w_b, wb, half_b, 48, b_send, b_recv, 0, 1),
        slab(w_b, wb, half_b, 48, b_send, b_recv, 1, -1),
        slab(w_b, wb, half_b, 32, b_send, b_recv, 2, 2),
        slab(w_b, wb, half_b + 32, 16, b_send, b_recv, 3, -2),
    ]
    for copy in copies_b:
        copy.start()

    copies_fx = []
    copies_fy = []

    def share_y(k, px):
        made = [
            remote(f_far.at[piece(px)], f_far.at[piece(px)], fy_send.at[k, i], fy_recv.at[k, i], dy=dy)
            for i, dy in enumerate((1, -1, 2))
        ]
        for copy in made:
            copy.start()
        copies_fy.extend(made)

    cross.wait_recv()
    for k, dx in enumerate((1, -1, 2)):
        copy = remote(f_far.at[piece(x)], f_far.at[piece(x)], fx_send.at[k], fx_recv.at[k], dx=dx)
        copy.start()
        copies_fx.append(copy)
    share_y(0, x)

    copies_bs = to_sibling(wb, half_b, OROWS // 2, bs_send, bs_recv)
    for copy in copies_b:
        copy.wait_recv()
    for copy in copies_bs:
        copy.start()
    for k, dx in enumerate((-1, 1, 2)):
        copies_fx[k].wait_recv()
        share_y(k + 1, around(x, dx))
    local_b.wait()
    for copy in copies_bs:
        copy.wait_recv()
    for h in range(4):
        wo[h, 16 * h + 64 : 16 * h + 64 + OROWS, :] = wb[h]

    pl.when(has_prev)(seg_up.wait_recv)
    pl.when(has_next)(seg_down.wait_recv)
    for j in range(4):
        parts = [segs[b // 4, b % 4][:, :TOK] for b in range(j, j + 9)]
        seg_keys[j] = jnp.concatenate(parts, axis=1)
        mine = segs[1, j]
        spread = jnp.concatenate([mine] * 16, axis=0)
        seg_query[j] = jnp.transpose(spread)[:TOK]

    for up, down in copies_k:
        pl.when(has_prev)(up.wait_recv)
        pl.when(has_next)(down.wait_recv)

    scale = 1.0 / math.sqrt(HEAD)

    def attend(j):
        at = pl.ds(pl.multiple_of(j * TOK, TOK), TOK)
        window = pl.ds(pl.multiple_of(j * TOK, TOK), WINDOW)
        same = seg_query[j][:, 0:1] == seg_keys[j][0:1, :]
        total = None
        for h in range(4):
            scores = lax.dot_general(
                qs[at, 128 * h : 128 * h + 128],
                kv[window, 128 * h : 128 * h + 128],
                NT,
                preferred_element_type=F32,
            )
            scores = jnp.where(same, scores, -jnp.inf)
            top = jnp.max(scores, -1, keepdims=True)
            expo = jnp.exp((scores - top) * scale)
            weight = jnp.sum(expo, -1, keepdims=True)
            mixed = jnp.dot(
                expo.astype(BF16), kv[window, 128 * h : 128 * h + 256], preferred_element_type=F32
            )
            mixed = (mixed / weight).astype(BF16)
            term = jnp.dot(mixed, wo[h], preferred_element_type=F32)
            total = term if total is None else total + term
        return total

    def send_part(k, px):
        return pltpu.make_async_remote_copy(
            src_ref=part_out.at[k],
            dst_ref=part_in.at[k],
            send_sem=r_send.at[k],
            recv_sem=r_recv.at[k],
            device_id={"zl": zl, "x": px, "y": y, "zh": zh, "c": c},
            device_id_type=MESH_ID,
        )

    def attend_step(k, carry):
        j = around(x, k + 1)
        total = attend(j)

        @pl.when(k < 3)
        def _():
            part_out[k] = total.astype(BF16)
            send_part(k, j).start()

        @pl.when(k == 3)
        def _():
            own_part[...] = total

        return carry

    lax.fori_loop(0, 4, attend_step, 0)

    attended = emb[...] + own_part[...] + vecs[4:5, :]
    for k in range(3):
        send_part(k, around(x, k + 1)).wait_recv()
        attended = attended + part_in[k].astype(F32)
    own_part[...] = attended
    n2[c] = norm_rows(attended, vecs[2:3, :], vecs[3:4, :]).astype(BF16)
    give = remote(n2.at[c], n2.at[c], m_send.at[0], m_recv.at[0], dc=1)
    give.start()
    local_f.wait()
    give.wait_recv()

    tokens = n2[...].reshape(2 * TOK, WIDTH)

    def hidden_of(weights, biases):
        def step(i, carry):
            at = pl.ds(pl.multiple_of(i * 384, 384), 384)
            inner = jnp.dot(tokens, weights[0:WIDTH, at], preferred_element_type=F32)
            hid[:, at] = gelu(inner + biases[6:7, at]).astype(BF16)
            return carry

        lax.fori_loop(0, 3, step, 0)

    def project_hidden(weights, first):
        def step(i, carry):
            at = pl.ds(pl.multiple_of(i * 384, 384), 384)
            got = jnp.dot(hid[...], weights[WIDTH : 2 * WIDTH, at], preferred_element_type=F32)
            mlp[:, at] = got if first else mlp[:, at] + got
            return carry

        lax.fori_loop(0, 3, step, 0)

    hidden_of(f_own, vecs)
    project_hidden(f_own, True)
    for copy in copies_fy:
        copy.wait_recv()
    cross_v.wait_recv()
    hidden_of(f_far, vecs_far)
    project_hidden(f_far, False)

    mine_at = pl.ds(pl.multiple_of(c * TOK, TOK), TOK)
    other_at = pl.ds(pl.multiple_of((1 - c) * TOK, TOK), TOK)
    mlp_out[...] = mlp[other_at, :].astype(BF16)
    back = remote(mlp_out, mlp_in, m_send.at[1], m_recv.at[1], dc=1)
    back.start()
    mine_sum = own_part[...] + vecs[5:6, :] + mlp[mine_at, :]
    back.wait_recv()
    out[...] = (mine_sum + mlp_in[...].astype(F32)).astype(BF16)

    for copy in copies_a + copies_as + copies_n + copies_s + copies_b + copies_bs:
        copy.wait_send()
    for up, down in copies_k:
        pl.when(has_next)(up.wait_send)
        pl.when(has_prev)(down.wait_send)
    pl.when(has_next)(seg_up.wait_send)
    pl.when(has_prev)(seg_down.wait_send)
    for copy in [cross, cross_v, give, back] + copies_fx + copies_fy:
        copy.wait_send()
    for k in range(3):
        send_part(k, around(x, k + 1)).wait_send()


def layer_call(*operands):
    vmem = pl.BlockSpec(memory_space=pltpu.VMEM)
    hbm = pl.BlockSpec(memory_space=pl.ANY)
    dma = pltpu.SemaphoreType.DMA
    scratch = [
        pltpu.VMEM((TOK, WIDTH), F32),
        pltpu.VMEM((4, TOK, WIDTH), BF16),
        pltpu.VMEM((3, 4, 8, 256), F32),
        pltpu.VMEM((4, 8, WINDOW), F32),
        pltpu.VMEM((4, TOK, 128), F32),
        pltpu.VMEM((4, QROWS, WIDTH), BF16),
        pltpu.VMEM((4, OROWS, WIDTH), BF16),
        pltpu.VMEM((WIDTH, WIDTH), BF16),
        pltpu.VMEM((4, 256, WIDTH), BF16),
        pltpu.VMEM((ROW, 512), BF16),
        pltpu.VMEM((3 * ROW, 640), BF16),
        pltpu.VMEM((3, TOK, WIDTH), BF16),
        pltpu.VMEM((3, TOK, WIDTH), BF16),
        pltpu.VMEM((TOK, WIDTH), F32),
        pltpu.VMEM((2 * WIDTH, WIDTH), BF16),
        pltpu.VMEM((2 * WIDTH, WIDTH), BF16),
        pltpu.VMEM((8, WIDTH), F32),
        pltpu.VMEM((2, TOK, WIDTH), BF16),
        pltpu.VMEM((2 * TOK, WIDTH), BF16),
        pltpu.VMEM((2 * TOK, WIDTH), F32),
        pltpu.VMEM((TOK, WIDTH), BF16),
        pltpu.VMEM((TOK, WIDTH), BF16),
        dma((3,)),
    ]
    for shape in ((4,), (3,), (4,), (3,), (3,), (5,), (2, 4), (2,), (3,), (4, 3), (3,), (2,)):
        scratch += [dma(shape), dma(shape)]
    return pl.pallas_call(
        layer_kernel,
        out_shape=jax.ShapeDtypeStruct((TOK, WIDTH), BF16),
        in_specs=[vmem] * 5 + [hbm] * 3,
        out_specs=vmem,
        scratch_shapes=scratch,
        compiler_params=pltpu.CompilerParams(
            collective_id=0, has_side_effects=True, vmem_limit_bytes=60 << 20
        ),
        name="encoder_layer",
    )(*operands)


def per_device(
    patches,
    seg_ids,
    pos_rows,
    pos_cols,
    row_table,
    col_table,
    ln1_gain,
    ln1_bias,
    w_qkv,
    w_out,
    out_bias,
    ln2_gain,
    ln2_bias,
    w_fc1,
    fc1_bias,
    w_fc2,
    fc2_bias,
):
    ints = jnp.pad(jnp.concatenate([seg_ids, pos_rows, pos_cols], 0), ((0, 5), (0, 64)))
    pad_hidden = WIDTH - w_fc1.shape[1]
    vecs = jnp.stack(
        [
            ln1_gain,
            ln1_bias,
            ln2_gain,
            ln2_bias,
            out_bias.astype(F32),
            fc2_bias.astype(F32),
            jnp.pad(fc1_bias.astype(F32), (0, pad_hidden)),
            jnp.zeros_like(ln1_gain),
        ]
    )
    turned = w_qkv.T
    w_a = jnp.concatenate(
        [turned[:HEAD], jnp.zeros((8, WIDTH), BF16), turned[HEAD:]], axis=0
    )
    w_b = jnp.pad(w_out, ((8, OROWS - HEAD - 8), (0, 0)))
    w_f = jnp.concatenate(
        [jnp.pad(w_fc1, ((0, 0), (0, pad_hidden))), jnp.pad(w_fc2, ((0, pad_hidden), (0, 0)))],
        axis=0,
    )
    return layer_call(patches[0], ints, row_table, col_table, vecs, w_a, w_b, w_f)[None]


def solution(mesh):
    torus = Mesh(mesh.devices.reshape(4, 4, 4, 2, 2), AXES)
    in_specs = (
        P(BATCH, SEQ, None),
        P(BATCH, SEQ),
        P(BATCH, SEQ),
        P(BATCH, SEQ),
        P(),
        P(),
        P(),
        P(),
        P(None, SEQ),
        P(SEQ, None),
        P(),
        P(),
        P(),
        P(None, ("zh", "c")),
        P(("zh", "c")),
        P(("zh", "c"), None),
        P(),
    )
    return jax.shard_map(
        per_device,
        mesh=torus,
        in_specs=in_specs,
        out_specs=P(BATCH, SEQ, None),
        check_vma=False,
    )
```

```python
import math

import jax
import jax.numpy as jnp
from jax import lax
from jax.experimental import pallas as pl
from jax.experimental.pallas import tpu as pltpu
from jax.sharding import Mesh
from jax.sharding import PartitionSpec as P

AXES = ("zl", "x", "y", "zh", "c")
SEQ = ("zl", "x")
BATCH = ("y", "zh", "c")
MESH_ID = pl.DeviceIdType.MESH
TOK = 192
WIDTH = 1152
ROW = 4 * TOK
HEAD = 72
WINDOW = 9 * TOK
QROWS = 224
OROWS = 96
F32 = jnp.float32
BF16 = jnp.bfloat16
NT = (((1,), (1,)), ((), ()))


def norm_rows(values, gain, shift):
    center = jnp.mean(values, -1, keepdims=True)
    moved = values - center
    spread = jnp.mean(jnp.square(moved), -1, keepdims=True)
    return moved * lax.rsqrt(spread + 1e-06) * gain + shift


def gelu(u):
    return 0.5 * u * (1.0 + jnp.tanh(math.sqrt(2.0 / math.pi) * (u + 0.044715 * u * u * u)))


def layer_kernel(
    patches,
    seg_in,
    rows_in,
    cols_in,
    rows_tab,
    cols_tab,
    ln1_gain,
    ln1_bias,
    ln2_gain,
    ln2_bias,
    out_bias,
    fc2_bias,
    fc1_bias,
    w_a,
    w_b,
    w_1,
    w_2,
    w_tail,
    out,
    emb,
    nrm,
    segs,
    seg_keys,
    seg_query,
    wz,
    wb,
    wp,
    wo,
    qs,
    kv,
    part_out,
    part_in,
    own_part,
    f_own,
    f_far,
    bias_own,
    bias_far,
    stage_a,
    stage_b,
    ring_in,
    n2,
    hid,
    mlp,
    mlp_out,
    mlp_in,
    loc_sem,
    a_send,
    a_recv,
    as_send,
    as_recv,
    b_send,
    b_recv,
    bs_send,
    bs_recv,
    n_send,
    n_recv,
    s_send,
    s_recv,
    k_send,
    k_recv,
    f_send,
    f_recv,
    f1_send,
    f1_recv,
    f2_send,
    f2_recv,
    r_send,
    r_recv,
    m_send,
    m_recv,
):
    zl, x, y, zh, c = (lax.axis_index(a) for a in AXES)
    z = zh * 4 + zl

    def device(dz=0, dx=0, dy=0, dc=0, mirror=False):
        zz = 7 - z if mirror else lax.rem(z + dz + 8, 8)
        return {
            "zl": lax.rem(zz, 4),
            "x": lax.rem(x + dx + 4, 4),
            "y": lax.rem(y + dy + 4, 4),
            "zh": zz // 4,
            "c": lax.rem(c + dc, 2),
        }

    def remote(src, dst, send, recv, **where):
        return pltpu.make_async_remote_copy(
            src_ref=src,
            dst_ref=dst,
            send_sem=send,
            recv_sem=recv,
            device_id=device(**where),
            device_id_type=MESH_ID,
        )

    def around(v, d):
        return lax.rem(v + d + 4, 4)

    has_prev = zl > 0
    has_next = zl < 3

    barrier = pltpu.get_barrier_semaphore()
    peers = (
        [dict(dz=d) for d in (1, -1, 2, -2)]
        + [dict(dx=d) for d in (1, -1, 2)]
        + [dict(dy=d) for d in (1, -1, 2)]
        + [dict(dc=1), dict(mirror=True)]
    )
    for peer in peers:
        pl.semaphore_signal(barrier, inc=1, device_id=device(**peer), device_id_type=MESH_ID)

    local = [
        pltpu.make_async_copy(w_a, stage_a, loc_sem.at[0]),
        pltpu.make_async_copy(w_b, stage_b, loc_sem.at[1]),
        pltpu.make_async_copy(w_1.at[0:1024], f_own.at[0:1024], loc_sem.at[2]),
        pltpu.make_async_copy(w_2.at[0:1024], f_own.at[1152:2176], loc_sem.at[3]),
        pltpu.make_async_copy(w_tail.at[0:128], f_own.at[1024:1152], loc_sem.at[4]),
        pltpu.make_async_copy(w_tail.at[128:256], f_own.at[2176:2304], loc_sem.at[5]),
    ]
    for copy in local:
        copy.start()

    def wide(ref):
        return jnp.concatenate([ref[...].astype(F32), jnp.zeros((1, 64), F32)], axis=1)

    level = lax.broadcasted_iota(jnp.int32, (128, 256), 0).astype(F32)
    wanted = jnp.where(level < 64.0, wide(rows_in), wide(cols_in) + 64.0)
    hot = jnp.transpose(jnp.where(level == wanted, 1.0, 0.0))[:TOK].astype(BF16)
    tables = jnp.concatenate([rows_tab[...], cols_tab[...]], axis=0)
    embedded = patches[...].astype(F32) + jnp.dot(hot, tables, preferred_element_type=F32)
    emb[...] = embedded
    nrm[x] = norm_rows(embedded, ln1_gain[...], ln1_bias[...]).astype(BF16)
    segs[1, x] = jnp.broadcast_to(wide(seg_in), (8, 256))
    bias_own[...] = jnp.broadcast_to(fc1_bias[...], (8, WIDTH))

    local[0].wait()
    staged = stage_a[...].astype(F32)
    wz[zl] = jnp.concatenate(
        [staged[:HEAD], jnp.zeros((8, WIDTH), F32), staged[HEAD:]], axis=0
    ).astype(BF16)
    pl.semaphore_wait(barrier, len(peers))

    def slab(buf, first, rows, send, recv, k, dz):
        ref = buf.at[zl, pl.ds(pl.multiple_of(first, 16), rows)]
        return remote(ref, ref, send.at[k], recv.at[k], dz=dz)

    half_a = c * (QROWS // 2)
    copies_a = [
        slab(wz, half_a, 112, a_send, a_recv, 0, 1),
        slab(wz, half_a, 112, a_send, a_recv, 1, -1),
        slab(wz, half_a, 64, a_send, a_recv, 2, 2),
        slab(wz, half_a + 64, 48, a_send, a_recv, 3, -2),
    ]
    for copy in copies_a:
        copy.start()

    LOW, HIGH = pl.ds(0, 96), pl.ds(96, 96)
    copies_n = [
        remote(nrm.at[x], nrm.at[x], n_send.at[k], n_recv.at[k], dx=dx)
        for k, dx in enumerate((1, -1))
    ]
    copies_s = [
        remote(segs.at[1, x], segs.at[1, x], s_send.at[k], s_recv.at[k], dx=dx)
        for k, dx in enumerate((1, -1, 2))
    ]
    for copy in copies_n + copies_s:
        copy.start()

    def unit(py, px, first, rows):
        at = pl.multiple_of((py * 4 + px) * 144 + first, 16)
        return f_far.at[pl.ds(at, rows)]

    for copy in local[2:]:
        copy.wait()
    mine = pl.ds(pl.multiple_of((y * 4 + x) * 144, 16), 144)
    cross = remote(f_own.at[mine], f_far.at[mine], f_send.at[0], f_recv.at[0], mirror=True)
    cross_v = remote(bias_own, bias_far, f_send.at[1], f_recv.at[1], mirror=True)
    cross.start()
    cross_v.start()

    local[1].wait()
    wb[zl] = jnp.concatenate(
        [
            jnp.zeros((8, WIDTH), F32),
            stage_b[...].astype(F32),
            jnp.zeros((OROWS - HEAD - 8, WIDTH), F32),
        ],
        axis=0,
    ).astype(BF16)

    wp[...] = jnp.zeros_like(wp)
    wo[...] = jnp.zeros_like(wo)

    @pl.when(jnp.logical_not(has_prev))
    def _():
        kv[0:ROW, :] = jnp.zeros((ROW, 640), BF16)
        segs[0] = jnp.full((4, 8, 256), -1.0, F32)

    @pl.when(jnp.logical_not(has_next))
    def _():
        kv[2 * ROW : 3 * ROW, :] = jnp.zeros((ROW, 640), BF16)
        segs[2] = jnp.full((4, 8, 256), -1.0, F32)

    left, right, far_x = around(x, -1), around(x, 1), around(x, 2)
    copies_n[0].wait_recv()
    on_right = remote(nrm.at[left, LOW], nrm.at[left, LOW], n_send.at[2], n_recv.at[2], dx=1)
    on_right.start()
    copies_n[1].wait_recv()
    on_left = remote(nrm.at[right, HIGH], nrm.at[right, HIGH], n_send.at[3], n_recv.at[3], dx=-1)
    on_left.start()

    def to_sibling(buf, first, rows, send, recv):
        at = pl.ds(pl.multiple_of(first, 16), rows)
        made = []
        for k, d in enumerate((-1, 1, 2)):
            ref = buf.at[around(zl, d), at]
            made.append(remote(ref, ref, send.at[k], recv.at[k], dc=1))
        return made

    copies_as = to_sibling(wz, half_a, QROWS // 2, as_send, as_recv)
    for copy in copies_a:
        copy.wait_recv()
    for copy in copies_as:
        copy.start()
    for copy in copies_as:
        copy.wait_recv()
    for h in range(4):
        wp[144 * h : 144 * h + 80, :] = wz[h, 0:80, :]
        wp[512 + 144 * h : 656 + 144 * h, :] = wz[h, 80:QROWS, :]

    copies_k = []

    def project(k, source):
        tokens = nrm[source]
        at = pl.ds(pl.multiple_of(source * TOK, TOK), TOK)
        here = pl.ds(pl.multiple_of(ROW + source * TOK, TOK), TOK)
        as_next = pl.ds(pl.multiple_of(2 * ROW + source * TOK, TOK), TOK)
        kv[here, :] = lax.dot_general(
            tokens, wp[512:1152, :], NT, preferred_element_type=F32
        ).astype(BF16)
        up = remote(kv.at[here], kv.at[at], k_send.at[0, k], k_recv.at[0, k], dz=1)
        down = remote(kv.at[here], kv.at[as_next], k_send.at[1, k], k_recv.at[1, k], dz=-1)
        copies_k.append((up, down))
        pl.when(has_next)(up.start)
        pl.when(has_prev)(down.start)
        qs[at, :] = lax.dot_general(
            tokens, wp[0:512, :], NT, preferred_element_type=F32
        ).astype(BF16)

    project(0, x)
    project(1, left)
    project(2, right)

    PARTS = ((0, 80, 48), (80, 64, 32))
    def held(part, k, db=0):
        d = (0, -1, 1, 2)[k]
        if part == 0:
            return around(y, db), around(x, d)
        return around(y, d), around(x, db)

    def along(part, phase, d):
        return dict(dx=d) if (part == 0) == (phase == 0) else dict(dy=d)

    def first_copy(part, i):
        first, rows, _ = PARTS[part]
        ref = unit(y, x, first, rows)
        d = (1, -1, 2)[i]
        return remote(ref, ref, f1_send.at[part, i], f1_recv.at[part, i], **along(part, 0, d))

    def second_copy(part, k, i):
        first, rows, _ = PARTS[part]
        ref = unit(*held(part, k), first, rows)
        return remote(
            ref, ref, f2_send.at[part, k, i], f2_recv.at[part, k, i], **along(part, 1, (1, -1)[i])
        )

    def hand_copy(part, k, i):
        first, rows, half = PARTS[part]
        cut = ((first, half), (first + half, rows - half))[i]
        d = (1, -1)[i]
        ref = unit(*held(part, k, -d), *cut)
        at = (part, k, 2 + i)
        return remote(ref, ref, f2_send.at[at], f2_recv.at[at], **along(part, 1, d))

    def start_first(part):
        for i in range(3):
            first_copy(part, i).start()

    def start_second(part, k):
        for i in range(2):
            second_copy(part, k, i).start()

    def hand_on(part, k):
        for i in range(2):
            second_copy(part, k, i).wait_recv()
            hand_copy(part, k, i).start()

    cross.wait_recv()
    for part in (0, 1):
        start_first(part)
        start_second(part, 0)

    on_right.wait_recv()
    on_left.wait_recv()
    project(3, far_x)
    for copy in copies_s:
        copy.wait_recv()
    seg_up = remote(segs.at[1], segs.at[0], s_send.at[3], s_recv.at[3], dz=1)
    seg_down = remote(segs.at[1], segs.at[2], s_send.at[4], s_recv.at[4], dz=-1)
    pl.when(has_next)(seg_up.start)
    pl.when(has_prev)(seg_down.start)

    half_b = c * (OROWS // 2)
    copies_b = [
        slab(wb, half_b, 48, b_send, b_recv, 0, 1),
        slab(wb, half_b, 48, b_send, b_recv, 1, -1),
        slab(wb, half_b, 32, b_send, b_recv, 2, 2),
        slab(wb, half_b + 32, 16, b_send, b_recv, 3, -2),
    ]
    for copy in copies_b:
        copy.start()

    for k in (1, 2, 3):
        for part in (1, 0):
            first_copy(part, k - 1).wait_recv()
            start_second(part, k)
    for part in (1, 0):
        hand_on(part, 0)

    copies_bs = to_sibling(wb, half_b, OROWS // 2, bs_send, bs_recv)
    for copy in copies_b:
        copy.wait_recv()
    for copy in copies_bs:
        copy.start()

    pl.when(has_prev)(seg_up.wait_recv)
    pl.when(has_next)(seg_down.wait_recv)
    for j in range(4):
        parts = [segs[b // 4, b % 4][:, :TOK] for b in range(j, j + 9)]
        seg_keys[j] = jnp.concatenate(parts, axis=1)
        mine_seg = segs[1, j]
        spread = jnp.concatenate([mine_seg] * 16, axis=0)
        seg_query[j] = jnp.transpose(spread)[:TOK]
    for copy in copies_bs:
        copy.wait_recv()
    for h in range(4):
        wo[h, 16 * h + 64 : 16 * h + 64 + OROWS, :] = wb[h]

    for up, down in copies_k:
        pl.when(has_prev)(up.wait_recv)
        pl.when(has_next)(down.wait_recv)

    scale = 1.0 / math.sqrt(HEAD)

    def attend(j):
        at = pl.ds(pl.multiple_of(j * TOK, TOK), TOK)
        window = pl.ds(pl.multiple_of(j * TOK, TOK), WINDOW)
        same = seg_query[j][:, 0:1] == seg_keys[j][0:1, :]
        total = None
        for h in range(4):
            scores = lax.dot_general(
                qs[at, 128 * h : 128 * h + 128],
                kv[window, 128 * h : 128 * h + 128],
                NT,
                preferred_element_type=F32,
            )
            scores = jnp.where(same, scores, -jnp.inf)
            top = jnp.max(scores, -1, keepdims=True)
            expo = jnp.exp((scores - top) * scale)
            weight = jnp.sum(expo, -1, keepdims=True)
            mixed = jnp.dot(
                expo.astype(BF16), kv[window, 128 * h : 128 * h + 256], preferred_element_type=F32
            )
            mixed = (mixed / weight).astype(BF16)
            term = jnp.dot(mixed, wo[h], preferred_element_type=F32)
            total = term if total is None else total + term
        return total

    def half_right():
        return remote(part_out.at[0, LOW], ring_in.at[0], r_send.at[0], r_recv.at[0], dx=1)

    def half_left():
        return remote(part_out.at[0, HIGH], ring_in.at[1], r_send.at[1], r_recv.at[1], dx=-1)

    def to_right():
        return remote(part_out.at[1], part_in.at[0], r_send.at[2], r_recv.at[2], dx=1)

    def to_left():
        return remote(part_out.at[2], part_in.at[1], r_send.at[3], r_recv.at[3], dx=-1)

    def attend_step(k, carry):
        d = jnp.where(k == 0, 2, jnp.where(k == 1, 1, jnp.where(k == 2, 3, 0)))
        own_part[...] = attend(around(x, d))

        @pl.when(k == 0)
        def _():
            part_out[0] = own_part[...].astype(BF16)
            half_right().start()
            half_left().start()
            for part in (1, 0):
                hand_on(part, 1)

        @pl.when(k == 1)
        def _():
            half_right().wait_recv()
            part_out[1, LOW] = (own_part[LOW, :] + ring_in[0].astype(F32)).astype(BF16)
            part_out[1, HIGH] = own_part[HIGH, :].astype(BF16)
            to_right().start()
            for part in (1, 0):
                hand_on(part, 2)

        @pl.when(k == 2)
        def _():
            half_left().wait_recv()
            part_out[2, LOW] = own_part[LOW, :].astype(BF16)
            part_out[2, HIGH] = (own_part[HIGH, :] + ring_in[1].astype(F32)).astype(BF16)
            to_left().start()
            for part in (1, 0):
                hand_on(part, 3)

        return carry

    lax.fori_loop(0, 4, attend_step, 0)

    attended = emb[...] + own_part[...] + out_bias[...].astype(F32)
    to_right().wait_recv()
    attended = attended + part_in[0].astype(F32)
    to_left().wait_recv()
    attended = attended + part_in[1].astype(F32)
    own_part[...] = attended
    n2[c] = norm_rows(attended, ln2_gain[...], ln2_bias[...]).astype(BF16)
    give = remote(n2.at[c], n2.at[c], m_send.at[0], m_recv.at[0], dc=1)
    give.start()
    give.wait_recv()

    tokens = n2[...].reshape(2 * TOK, WIDTH)

    def hidden_of(weights, biases):
        def step(i, carry):
            at = pl.ds(pl.multiple_of(i * 384, 384), 384)
            inner = lax.dot_general(tokens, weights[at, :], NT, preferred_element_type=F32)
            hid[:, at] = gelu(inner + biases[0:1, at]).astype(BF16)
            return carry

        lax.fori_loop(0, 3, step, 0)

    def project_hidden(weights, first):
        def step(i, carry):
            at = pl.ds(pl.multiple_of(i * 384, 384), 384)
            got = jnp.dot(hid[...], weights[WIDTH : 2 * WIDTH, at], preferred_element_type=F32)
            mlp[:, at] = got if first else mlp[:, at] + got
            return carry

        lax.fori_loop(0, 3, step, 0)

    hidden_of(f_own, bias_own)
    project_hidden(f_own, True)
    for part in (0, 1):
        for k in range(4):
            for i in range(2):
                hand_copy(part, k, i).wait_recv()
    cross_v.wait_recv()
    hidden_of(f_far, bias_far)
    project_hidden(f_far, False)

    mine_at = pl.ds(pl.multiple_of(c * TOK, TOK), TOK)
    other_at = pl.ds(pl.multiple_of((1 - c) * TOK, TOK), TOK)
    mlp_out[...] = mlp[other_at, :].astype(BF16)
    back = remote(mlp_out, mlp_in, m_send.at[1], m_recv.at[1], dc=1)
    back.start()
    mine_sum = own_part[...] + fc2_bias[...].astype(F32) + mlp[mine_at, :]
    back.wait_recv()
    out[...] = (mine_sum + mlp_in[...].astype(F32)).astype(BF16)

    for copy in copies_a + copies_as + copies_n + copies_s + copies_b + copies_bs:
        copy.wait_send()
    for up, down in copies_k:
        pl.when(has_next)(up.wait_send)
        pl.when(has_prev)(down.wait_send)
    pl.when(has_next)(seg_up.wait_send)
    pl.when(has_prev)(seg_down.wait_send)
    for copy in [cross, cross_v, give, back, on_right, on_left]:
        copy.wait_send()
    for copy in [half_right(), half_left(), to_right(), to_left()]:
        copy.wait_send()
    for part in (0, 1):
        for i in range(3):
            first_copy(part, i).wait_send()
        for k in range(4):
            for i in range(2):
                second_copy(part, k, i).wait_send()
                hand_copy(part, k, i).wait_send()


def layer_call(*operands):
    vmem = pl.BlockSpec(memory_space=pltpu.VMEM)
    hbm = pl.BlockSpec(memory_space=pl.ANY)
    dma = pltpu.SemaphoreType.DMA
    scratch = [
        pltpu.VMEM((TOK, WIDTH), F32),
        pltpu.VMEM((4, TOK, WIDTH), BF16),
        pltpu.VMEM((3, 4, 8, 256), F32),
        pltpu.VMEM((4, 8, WINDOW), F32),
        pltpu.VMEM((4, TOK, 128), F32),
        pltpu.VMEM((4, QROWS, WIDTH), BF16),
        pltpu.VMEM((4, OROWS, WIDTH), BF16),
        pltpu.VMEM((WIDTH, WIDTH), BF16),
        pltpu.VMEM((4, 256, WIDTH), BF16),
        pltpu.VMEM((ROW, 512), BF16),
        pltpu.VMEM((3 * ROW, 640), BF16),
        pltpu.VMEM((3, TOK, WIDTH), BF16),
        pltpu.VMEM((2, TOK, WIDTH), BF16),
        pltpu.VMEM((TOK, WIDTH), F32),
        pltpu.VMEM((2 * WIDTH, WIDTH), BF16),
        pltpu.VMEM((2 * WIDTH, WIDTH), BF16),
        pltpu.VMEM((8, WIDTH), F32),
        pltpu.VMEM((8, WIDTH), F32),
        pltpu.VMEM((3 * HEAD, WIDTH), BF16),
        pltpu.VMEM((HEAD, WIDTH), BF16),
        pltpu.VMEM((2, 96, WIDTH), BF16),
        pltpu.VMEM((2, TOK, WIDTH), BF16),
        pltpu.VMEM((2 * TOK, WIDTH), BF16),
        pltpu.VMEM((2 * TOK, WIDTH), F32),
        pltpu.VMEM((TOK, WIDTH), BF16),
        pltpu.VMEM((TOK, WIDTH), BF16),
        dma((6,)),
    ]
    for shape in ((4,), (3,), (4,), (3,), (4,), (5,), (2, 4), (2,), (2, 3), (2, 4, 4), (4,), (2,)):
        scratch += [dma(shape), dma(shape)]
    return pl.pallas_call(
        layer_kernel,
        out_shape=jax.ShapeDtypeStruct((TOK, WIDTH), BF16),
        in_specs=[vmem] * 13 + [hbm] * 5,
        out_specs=vmem,
        scratch_shapes=scratch,
        compiler_params=pltpu.CompilerParams(
            collective_id=0, has_side_effects=True, vmem_limit_bytes=60 << 20
        ),
        name="encoder_layer",
    )(*operands)


def per_device(
    patches,
    seg_ids,
    pos_rows,
    pos_cols,
    row_table,
    col_table,
    ln1_gain,
    ln1_bias,
    w_qkv,
    w_out,
    out_bias,
    ln2_gain,
    ln2_bias,
    w_fc1,
    fc1_bias,
    w_fc2,
    fc2_bias,
):
    rest = w_fc2.shape[0] - 1024
    w_1 = w_fc1.T
    w_tail = jnp.concatenate(
        [jnp.pad(w[1024:], ((0, 128 - rest), (0, 0))) for w in (w_1, w_fc2)], axis=0
    )
    return layer_call(
        patches[0],
        seg_ids,
        pos_rows,
        pos_cols,
        row_table,
        col_table,
        ln1_gain[None],
        ln1_bias[None],
        ln2_gain[None],
        ln2_bias[None],
        out_bias[None],
        fc2_bias[None],
        jnp.pad(fc1_bias.astype(F32), (0, WIDTH - fc1_bias.shape[0]))[None],
        w_qkv.T,
        w_out,
        w_1,
        w_fc2,
        w_tail,
    )[None]


def solution(mesh):
    torus = Mesh(mesh.devices.reshape(4, 4, 4, 2, 2), AXES)
    in_specs = (
        P(BATCH, SEQ, None),
        P(BATCH, SEQ),
        P(BATCH, SEQ),
        P(BATCH, SEQ),
        P(),
        P(),
        P(),
        P(),
        P(None, SEQ),
        P(SEQ, None),
        P(),
        P(),
        P(),
        P(None, ("zh", "c")),
        P(("zh", "c")),
        P(("zh", "c"), None),
        P(),
    )
    return jax.shard_map(
        per_device,
        mesh=torus,
        in_specs=in_specs,
        out_specs=P(BATCH, SEQ, None),
        check_vma=False,
    )
```

```python
import math

import jax
import jax.numpy as jnp
from jax import lax
from jax.experimental import pallas as pl
from jax.experimental.pallas import tpu as pltpu
from jax.sharding import Mesh
from jax.sharding import PartitionSpec as P

AXES = ("zl", "x", "y", "zh", "c")
SEQ = ("zl", "x")
BATCH = ("y", "zh", "c")
MESH_ID = pl.DeviceIdType.MESH
TOK = 192
WIDTH = 1152
ROW = 4 * TOK
HEAD = 72
QROWS = 224
F32 = jnp.float32
BF16 = jnp.bfloat16
NT = (((1,), (1,)), ((), ()))


def norm_rows(values, gain, shift):
    center = jnp.mean(values, -1, keepdims=True)
    moved = values - center
    spread = jnp.mean(jnp.square(moved), -1, keepdims=True)
    return moved * lax.rsqrt(spread + 1e-06) * gain + shift


def line(ref):
    return ref[...].astype(F32).reshape(1, WIDTH)


def gelu(u):
    return 0.5 * u * (1.0 + jnp.tanh(math.sqrt(2.0 / math.pi) * (u + 0.044715 * u * u * u)))


def layer_kernel(
    patches,
    seg_in,
    rows_in,
    cols_in,
    rows_tab,
    cols_tab,
    ln1_gain,
    ln1_bias,
    ln2_gain,
    ln2_bias,
    out_bias,
    fc2_bias,
    fc1_bias,
    w_a,
    w_b,
    w_1,
    w_2,
    tail_1,
    tail_2,
    out,
    emb,
    nrm,
    segs,
    seg_keys,
    seg_query,
    wz,
    wp,
    wof,
    pick,
    mixed_out,
    mixed_in,
    top_own,
    sum_own,
    mix_own,
    qs,
    kv,
    own_part,
    f_own,
    f_far,
    bias_own,
    bias_far,
    stage_a,
    stage_b,
    n2,
    hid,
    mlp,
    mlp_out,
    mlp_in,
    loc_sem,
    a_send,
    a_recv,
    as_send,
    as_recv,
    b_send,
    b_recv,
    bs_send,
    bs_recv,
    n_send,
    n_recv,
    s_send,
    s_recv,
    k_send,
    k_recv,
    f_send,
    f_recv,
    f1_send,
    f1_recv,
    f2_send,
    f2_recv,
    bx_send,
    bx_recv,
    r_send,
    r_recv,
    m_send,
    m_recv,
):
    zl, x, y, zh, c = (lax.axis_index(a) for a in AXES)
    z = zh * 4 + zl

    def device(dz=0, dx=0, dy=0, dc=0, mirror=False):
        zz = 7 - z if mirror else lax.rem(z + dz + 8, 8)
        return {
            "zl": lax.rem(zz, 4),
            "x": lax.rem(x + dx + 4, 4),
            "y": lax.rem(y + dy + 4, 4),
            "zh": zz // 4,
            "c": lax.rem(c + dc, 2),
        }

    def remote(src, dst, send, recv, **where):
        return pltpu.make_async_remote_copy(
            src_ref=src,
            dst_ref=dst,
            send_sem=send,
            recv_sem=recv,
            device_id=device(**where),
            device_id_type=MESH_ID,
        )

    def around(v, d):
        return lax.rem(v + d + 4, 4)

    has_prev = zl > 0
    has_next = zl < 3

    barrier = pltpu.get_barrier_semaphore()
    peers = (
        [dict(dz=d) for d in (1, -1, 2, -2)]
        + [dict(dx=d) for d in (1, -1, 2)]
        + [dict(dy=d) for d in (1, -1, 2)]
        + [dict(dc=1), dict(mirror=True)]
    )
    for peer in peers:
        pl.semaphore_signal(barrier, inc=1, device_id=device(**peer), device_id_type=MESH_ID)

    local = [
        pltpu.make_async_copy(w_a, stage_a, loc_sem.at[0]),
        pltpu.make_async_copy(w_b, stage_b, loc_sem.at[1]),
        pltpu.make_async_copy(w_1.at[0:1024], f_own.at[0:1024], loc_sem.at[2]),
        pltpu.make_async_copy(w_2.at[0:1024], f_own.at[1152:2176], loc_sem.at[3]),
    ]
    for copy in local:
        copy.start()

    local[0].wait()
    staged = stage_a[...].astype(F32)
    wz[zl] = jnp.concatenate(
        [staged[:HEAD], jnp.zeros((8, WIDTH), F32), staged[HEAD:]], axis=0
    ).astype(BF16)
    pl.semaphore_wait(barrier, len(peers))

    def slab(buf, first, rows, send, recv, k, dz):
        ref = buf.at[zl, pl.ds(pl.multiple_of(first, 16), rows)]
        return remote(ref, ref, send.at[k], recv.at[k], dz=dz)

    half_a = c * (QROWS // 2)
    copies_a = [
        slab(wz, half_a, 112, a_send, a_recv, 0, 1),
        slab(wz, half_a, 112, a_send, a_recv, 1, -1),
        slab(wz, half_a, 64, a_send, a_recv, 2, 2),
        slab(wz, half_a + 64, 48, a_send, a_recv, 3, -2),
    ]
    for copy in copies_a:
        copy.start()

    def wide(ref):
        return jnp.concatenate([ref[...].astype(F32), jnp.zeros((1, 64), F32)], axis=1)

    level = lax.broadcasted_iota(jnp.int32, (128, 256), 0).astype(F32)
    wanted = jnp.where(level < 64.0, wide(rows_in), wide(cols_in) + 64.0)
    hot = jnp.transpose(jnp.where(level == wanted, 1.0, 0.0))[:TOK].astype(BF16)
    tables = jnp.concatenate([rows_tab[...], cols_tab[...]], axis=0)
    embedded = patches[...].astype(F32) + jnp.dot(hot, tables, preferred_element_type=F32)
    emb[...] = embedded
    nrm[x] = norm_rows(embedded, line(ln1_gain), line(ln1_bias)).astype(BF16)
    segs[1, x] = jnp.broadcast_to(wide(seg_in), (8, 256))
    bias_own[...] = jnp.broadcast_to(line(fc1_bias), (8, WIDTH))

    LOW, HIGH = pl.ds(0, 96), pl.ds(96, 96)
    copies_n = [
        remote(nrm.at[x], nrm.at[x], n_send.at[k], n_recv.at[k], dx=dx)
        for k, dx in enumerate((1, -1))
    ]
    copies_s = [
        remote(segs.at[1, x], segs.at[1, x], s_send.at[k], s_recv.at[k], dx=dx)
        for k, dx in enumerate((1, -1, 2))
    ]
    for copy in copies_n + copies_s:
        copy.start()

    def unit(py, px, first, rows):
        at = pl.multiple_of((py * 4 + px) * 144 + first, 16)
        return f_far.at[pl.ds(at, rows)]

    local[1].wait()
    wof[x, pl.ds(pl.multiple_of(zl * 80, 16), 80)] = jnp.concatenate(
        [stage_b[...].astype(F32), jnp.zeros((8, WIDTH), F32)], axis=0
    ).astype(BF16)

    wp[...] = jnp.zeros_like(wp)
    lane = lax.broadcasted_iota(jnp.int32, (256, 384), 1)
    line_of = lax.broadcasted_iota(jnp.int32, (256, 384), 0)
    for h in range(4):
        feature = lane - 80 * h
        chosen = (line_of - (16 * h + HEAD) == feature) & (feature >= 0) & (feature < HEAD)
        pick[h] = jnp.where(chosen, 1.0, 0.0).astype(BF16)

    @pl.when(jnp.logical_not(has_prev))
    def _():
        kv[0:ROW, :] = jnp.zeros((ROW, 640), BF16)
        segs[0] = jnp.full((4, 8, 256), -1.0, F32)

    @pl.when(jnp.logical_not(has_next))
    def _():
        kv[ROW : 2 * ROW, :] = jnp.zeros((ROW, 640), BF16)
        segs[2] = jnp.full((4, 8, 256), -1.0, F32)

    left, right, far_x = around(x, -1), around(x, 1), around(x, 2)
    copies_n[0].wait_recv()
    on_right = remote(nrm.at[left, LOW], nrm.at[left, LOW], n_send.at[2], n_recv.at[2], dx=1)
    on_right.start()
    copies_n[1].wait_recv()
    on_left = remote(nrm.at[right, HIGH], nrm.at[right, HIGH], n_send.at[3], n_recv.at[3], dx=-1)
    on_left.start()

    def to_sibling(buf, first, rows, send, recv):
        at = pl.ds(pl.multiple_of(first, 16), rows)
        made = []
        for k, d in enumerate((-1, 1, 2)):
            ref = buf.at[around(zl, d), at]
            made.append(remote(ref, ref, send.at[k], recv.at[k], dc=1))
        return made

    copies_as = to_sibling(wz, half_a, QROWS // 2, as_send, as_recv)
    for copy in copies_a:
        copy.wait_recv()
    for copy in copies_as:
        copy.start()
    for copy in copies_as:
        copy.wait_recv()
    for h in range(4):
        wp[144 * h : 144 * h + 80, :] = wz[h, 0:80, :]
        wp[512 + 144 * h : 656 + 144 * h, :] = wz[h, 80:QROWS, :]

    copies_k = []

    def project(k, source):
        tokens = nrm[source]
        at = pl.ds(pl.multiple_of(source * TOK, TOK), TOK)
        here = pl.ds(pl.multiple_of(2 * ROW + source * TOK, TOK), TOK)
        as_next = pl.ds(pl.multiple_of(ROW + source * TOK, TOK), TOK)
        kv[here, :] = lax.dot_general(
            tokens, wp[512:1152, :], NT, preferred_element_type=F32
        ).astype(BF16)
        up = remote(kv.at[here], kv.at[at], k_send.at[0, k], k_recv.at[0, k], dz=1)
        down = remote(kv.at[here], kv.at[as_next], k_send.at[1, k], k_recv.at[1, k], dz=-1)
        copies_k.append((up, down))
        pl.when(has_next)(up.start)
        pl.when(has_prev)(down.start)
        qs[at, :] = lax.dot_general(
            tokens, wp[0:512, :], NT, preferred_element_type=F32
        ).astype(BF16)

    for copy in local[2:]:
        copy.wait()
    rest = w_1.shape[0] - 1024
    mine = pl.ds(pl.multiple_of((y * 4 + x) * 144, 16), 144)
    cross = remote(f_own.at[mine], f_far.at[mine], f_send.at[0], f_recv.at[0], mirror=True)
    cross_v = remote(bias_own, bias_far, f_send.at[1], f_recv.at[1], mirror=True)
    real = lax.broadcasted_iota(jnp.int32, (128, WIDTH), 0) < rest
    f_own[1024:1152, :] = jnp.where(real, tail_1[...], jnp.zeros((128, WIDTH), BF16))
    f_own[2176:2304, :] = jnp.where(real, tail_2[...], jnp.zeros((128, WIDTH), BF16))
    cross.start()
    cross_v.start()

    project(0, x)
    project(1, left)
    project(2, right)

    PARTS = ((0, 96, 48), (96, 48, 32))
    def held(part, k, db=0):
        d = (0, -1, 1, 2)[k]
        if part == 0:
            return around(y, db), around(x, d)
        return around(y, d), around(x, db)

    def along(part, phase, d):
        return dict(dx=d) if (part == 0) == (phase == 0) else dict(dy=d)

    def first_copy(part, i):
        first, rows, _ = PARTS[part]
        ref = unit(y, x, first, rows)
        d = (1, -1, 2)[i]
        return remote(ref, ref, f1_send.at[part, i], f1_recv.at[part, i], **along(part, 0, d))

    def second_copy(part, k, i):
        first, rows, _ = PARTS[part]
        ref = unit(*held(part, k), first, rows)
        return remote(
            ref, ref, f2_send.at[part, k, i], f2_recv.at[part, k, i], **along(part, 1, (1, -1)[i])
        )

    def hand_copy(part, k, i):
        first, rows, half = PARTS[part]
        cut = ((first, half), (first + half, rows - half))[i]
        d = (1, -1)[i]
        ref = unit(*held(part, k, -d), *cut)
        at = (part, k, 2 + i)
        return remote(ref, ref, f2_send.at[at], f2_recv.at[at], **along(part, 1, d))

    def start_first(part):
        for i in range(3):
            first_copy(part, i).start()

    def start_second(part, k):
        for i in range(2):
            second_copy(part, k, i).start()

    def hand_on(part, k):
        for i in range(2):
            second_copy(part, k, i).wait_recv()
            hand_copy(part, k, i).start()

    on_right.wait_recv()
    on_left.wait_recv()
    project(3, far_x)
    for copy in copies_s:
        copy.wait_recv()
    seg_up = remote(segs.at[1], segs.at[0], s_send.at[3], s_recv.at[3], dz=1)
    seg_down = remote(segs.at[1], segs.at[2], s_send.at[4], s_recv.at[4], dz=-1)
    pl.when(has_next)(seg_up.start)
    pl.when(has_prev)(seg_down.start)

    B_CUTS = ((0, 48), (48, 32))

    def rows_of(owner, core):
        first, rows = B_CUTS[core]
        return pl.ds(pl.multiple_of(owner * 80 + first, 16), rows)

    def b_copies(core):
        ref = wof.at[x, rows_of(zl, core)]
        return [
            remote(ref, ref, b_send.at[k], b_recv.at[k], dz=dz)
            for k, dz in enumerate((1, -1, (2, -2)[core]))
        ]

    def bs_copies(core):
        made = []
        for k, d in enumerate((-1, 1, 2)):
            ref = wof.at[x, rows_of(around(zl, d), core)]
            made.append(remote(ref, ref, bs_send.at[k], bs_recv.at[k], dc=1))
        return made

    def each_core(act):
        for core in (0, 1):

            @pl.when(c == core)
            def _():
                act(core)

    def start_b(core):
        for copy in b_copies(core):
            copy.start()

    def pass_b(core):
        for copy in b_copies(core):
            copy.wait_recv()
        for copy in bs_copies(core):
            copy.start()

    def take_b(core):
        for copy in bs_copies(1 - core):
            copy.wait_recv()

    def end_b(core):
        for copy in b_copies(core) + bs_copies(core):
            copy.wait_send()

    half_o = pl.ds(pl.multiple_of(c * 160, 16), 160)

    def bx_copy(k):
        ref = wof.at[x, half_o]
        return remote(ref, ref, bx_send.at[k], bx_recv.at[k], dx=(1, -1, 2)[k])

    def bxs_copy(k):
        ref = wof.at[around(x, (-1, 1, 2)[k]), half_o]
        return remote(ref, ref, bx_send.at[3 + k], bx_recv.at[3 + k], dc=1)

    each_core(start_b)

    cross.wait_recv()
    for part in (0, 1):
        start_first(part)
        start_second(part, 0)

    scale = 1.0 / math.sqrt(HEAD)
    seg_keys[0] = jnp.concatenate([segs[1, b][:, :TOK] for b in range(4)] + [segs[1, 0][:, :TOK]], axis=1)
    for j in range(4):
        spread = jnp.concatenate([segs[1, j]] * 16, axis=0)
        seg_query[j] = jnp.transpose(spread)[:TOK]

    def scores_of(j, h, keys):
        at = pl.ds(pl.multiple_of(j * TOK, TOK), TOK)
        return lax.dot_general(
            qs[at, 128 * h : 128 * h + 128],
            kv[keys, 128 * h : 128 * h + 128],
            NT,
            preferred_element_type=F32,
        )

    def attend_own(j):
        same = seg_query[j][:, 0:1] == seg_keys[0][0:1, :ROW]
        own = pl.ds(2 * ROW, ROW)
        for h in range(4):
            scores = jnp.where(same, scores_of(j, h, own), -jnp.inf)
            top = jnp.max(scores, -1, keepdims=True)
            expo = jnp.exp((scores - top) * scale)
            top_own[j, h] = jnp.broadcast_to(top, (TOK, 128))
            sum_own[j, h] = jnp.broadcast_to(jnp.sum(expo, -1, keepdims=True), (TOK, 128))
            mix_own[j, h] = jnp.dot(
                expo.astype(BF16), kv[own, 128 * h : 128 * h + 256], preferred_element_type=F32
            )

    def own_steps(first):
        def step(j, carry):
            attend_own(j)
            return carry

        lax.fori_loop(first, first + 2, step, 0)

    own_steps(0)
    for k in (1, 2, 3):
        for part in (1, 0):
            first_copy(part, k - 1).wait_recv()
            start_second(part, k)
    each_core(pass_b)
    each_core(take_b)
    for k in range(3):
        bx_copy(k).start()
    own_steps(2)
    for part in (1, 0):
        hand_on(part, 0)

    pl.when(has_prev)(seg_up.wait_recv)
    pl.when(has_next)(seg_down.wait_recv)
    around_segs = [segs[r, b][:, :TOK] for r in (0, 2) for b in range(4)]
    for j in range(4):
        seg_keys[j] = jnp.concatenate(around_segs[j : j + 5], axis=1)
    for up, down in copies_k:
        pl.when(has_prev)(up.wait_recv)
        pl.when(has_next)(down.wait_recv)

    def attend(j):
        window = pl.ds(pl.multiple_of(j * TOK, TOK), 5 * TOK)
        same = seg_query[j][:, 0:1] == seg_keys[j][0:1, :]
        total = None
        for h in range(4):
            scores = jnp.where(same, scores_of(j, h, window), -jnp.inf)
            before = top_own[j, h][:, 0:1]
            top = jnp.maximum(jnp.max(scores, -1, keepdims=True), before)
            expo = jnp.exp((scores - top) * scale)
            kept = jnp.exp((before - top) * scale)
            weight = jnp.sum(expo, -1, keepdims=True) + kept * sum_own[j, h][:, 0:1]
            mixed = jnp.dot(
                expo.astype(BF16), kv[window, 128 * h : 128 * h + 256], preferred_element_type=F32
            )
            mixed = ((mixed + kept * mix_own[j, h]) / weight).astype(BF16)
            term = jnp.dot(mixed, pick[h], preferred_element_type=F32)
            total = term if total is None else total + term
        return total.astype(BF16)

    def mixed_copy(k):
        return remote(
            mixed_out.at[k], mixed_in.at[k], r_send.at[k], r_recv.at[k], dx=(2, 1, -1)[k]
        )

    def attend_step(k, carry):
        d = jnp.where(k == 0, 2, jnp.where(k == 1, 1, jnp.where(k == 2, 3, 0)))
        got = attend(around(x, d))
        mixed_out[k] = got
        for step in range(3):

            @pl.when(k == step)
            def _():
                mixed_copy(step).start()
                for part in (1, 0):
                    hand_on(part, step + 1)
                bx_copy(step).wait_recv()
                bxs_copy(step).start()

        return carry

    lax.fori_loop(0, 4, attend_step, 0)

    def projected(held_in, px):
        return jnp.dot(held_in[:, 0:320], wof[px], preferred_element_type=F32)

    attended = emb[...] + projected(mixed_out[3], x) + line(out_bias)
    for k in range(3):
        bxs_copy(k).wait_recv()
    for k, d in enumerate((2, -1, 1)):
        mixed_copy(k).wait_recv()
        attended = attended + projected(mixed_in[k], around(x, d))
    own_part[...] = attended
    n2[c] = norm_rows(attended, line(ln2_gain), line(ln2_bias)).astype(BF16)
    give = remote(n2.at[c], n2.at[c], m_send.at[0], m_recv.at[0], dc=1)
    give.start()
    give.wait_recv()

    tokens = n2[...].reshape(2 * TOK, WIDTH)

    def hidden_of(weights, biases):
        def step(i, carry):
            at = pl.ds(pl.multiple_of(i * 384, 384), 384)
            inner = lax.dot_general(tokens, weights[at, :], NT, preferred_element_type=F32)
            hid[:, at] = gelu(inner + biases[0:1, at]).astype(BF16)
            return carry

        lax.fori_loop(0, 3, step, 0)

    def project_hidden(weights, first):
        def step(i, carry):
            at = pl.ds(pl.multiple_of(i * 384, 384), 384)
            got = jnp.dot(hid[...], weights[WIDTH : 2 * WIDTH, at], preferred_element_type=F32)
            mlp[:, at] = got if first else mlp[:, at] + got
            return carry

        lax.fori_loop(0, 3, step, 0)

    hidden_of(f_own, bias_own)
    project_hidden(f_own, True)
    for part in (0, 1):
        for k in range(4):
            for i in range(2):
                hand_copy(part, k, i).wait_recv()
    cross_v.wait_recv()
    hidden_of(f_far, bias_far)
    project_hidden(f_far, False)

    mine_at = pl.ds(pl.multiple_of(c * TOK, TOK), TOK)
    other_at = pl.ds(pl.multiple_of((1 - c) * TOK, TOK), TOK)
    mlp_out[...] = mlp[other_at, :].astype(BF16)
    back = remote(mlp_out, mlp_in, m_send.at[1], m_recv.at[1], dc=1)
    back.start()
    mine_sum = own_part[...] + line(fc2_bias) + mlp[mine_at, :]
    back.wait_recv()
    out[...] = (mine_sum + mlp_in[...].astype(F32)).astype(BF16)

    for copy in copies_a + copies_as + copies_n + copies_s:
        copy.wait_send()
    for up, down in copies_k:
        pl.when(has_next)(up.wait_send)
        pl.when(has_prev)(down.wait_send)
    pl.when(has_next)(seg_up.wait_send)
    pl.when(has_prev)(seg_down.wait_send)
    for copy in [cross, cross_v, give, back, on_right, on_left]:
        copy.wait_send()
    each_core(end_b)
    for k in range(3):
        bx_copy(k).wait_send()
        bxs_copy(k).wait_send()
        mixed_copy(k).wait_send()
    for part in (0, 1):
        for i in range(3):
            first_copy(part, i).wait_send()
        for k in range(4):
            for i in range(2):
                second_copy(part, k, i).wait_send()
                hand_copy(part, k, i).wait_send()


def layer_call(*operands):
    vmem = pl.BlockSpec(memory_space=pltpu.VMEM)
    hbm = pl.BlockSpec(memory_space=pl.ANY)
    edge = pl.BlockSpec((128, WIDTH), lambda i: (8, 0))
    dma = pltpu.SemaphoreType.DMA
    scratch = [
        pltpu.VMEM((TOK, WIDTH), F32),
        pltpu.VMEM((4, TOK, WIDTH), BF16),
        pltpu.VMEM((3, 4, 8, 256), F32),
        pltpu.VMEM((4, 8, 5 * TOK), F32),
        pltpu.VMEM((4, TOK, 128), F32),
        pltpu.VMEM((4, QROWS, WIDTH), BF16),
        pltpu.VMEM((WIDTH, WIDTH), BF16),
        pltpu.VMEM((4, 320, WIDTH), BF16),
        pltpu.VMEM((4, 256, 384), BF16),
        pltpu.VMEM((4, TOK, 384), BF16),
        pltpu.VMEM((3, TOK, 384), BF16),
        pltpu.VMEM((4, 4, TOK, 128), F32),
        pltpu.VMEM((4, 4, TOK, 128), F32),
        pltpu.VMEM((4, 4, TOK, 256), F32),
        pltpu.VMEM((ROW, 512), BF16),
        pltpu.VMEM((3 * ROW, 640), BF16),
        pltpu.VMEM((TOK, WIDTH), F32),
        pltpu.VMEM((2 * WIDTH, WIDTH), BF16),
        pltpu.VMEM((2 * WIDTH, WIDTH), BF16),
        pltpu.VMEM((8, WIDTH), F32),
        pltpu.VMEM((8, WIDTH), F32),
        pltpu.VMEM((3 * HEAD, WIDTH), BF16),
        pltpu.VMEM((HEAD, WIDTH), BF16),
        pltpu.VMEM((2, TOK, WIDTH), BF16),
        pltpu.VMEM((2 * TOK, WIDTH), BF16),
        pltpu.VMEM((2 * TOK, WIDTH), F32),
        pltpu.VMEM((TOK, WIDTH), BF16),
        pltpu.VMEM((TOK, WIDTH), BF16),
        dma((4,)),
    ]
    for shape in ((4,), (3,), (4,), (3,), (4,), (5,), (2, 4), (2,), (2, 3), (2, 4, 4), (6,), (3,), (2,)):
        scratch += [dma(shape), dma(shape)]
    return pl.pallas_call(
        layer_kernel,
        out_shape=jax.ShapeDtypeStruct((TOK, WIDTH), BF16),
        grid=(1,),
        in_specs=[vmem] * 13 + [hbm] * 4 + [edge] * 2,
        out_specs=vmem,
        scratch_shapes=scratch,
        compiler_params=pltpu.CompilerParams(
            collective_id=0, has_side_effects=True, vmem_limit_bytes=60 << 20
        ),
        name="encoder_layer",
    )(*operands)


def per_device(
    patches,
    seg_ids,
    pos_rows,
    pos_cols,
    row_table,
    col_table,
    ln1_gain,
    ln1_bias,
    w_qkv,
    w_out,
    out_bias,
    ln2_gain,
    ln2_bias,
    w_fc1,
    fc1_bias,
    w_fc2,
    fc2_bias,
):
    w_1 = w_fc1.T
    return layer_call(
        patches[0],
        seg_ids,
        pos_rows,
        pos_cols,
        row_table,
        col_table,
        ln1_gain,
        ln1_bias,
        ln2_gain,
        ln2_bias,
        out_bias,
        fc2_bias,
        jnp.pad(fc1_bias, (0, WIDTH - fc1_bias.shape[0])),
        w_qkv.T,
        w_out,
        w_1,
        w_fc2,
        w_1,
        w_fc2,
    )[None]


def solution(mesh):
    torus = Mesh(mesh.devices.reshape(4, 4, 4, 2, 2), AXES)
    in_specs = (
        P(BATCH, SEQ, None),
        P(BATCH, SEQ),
        P(BATCH, SEQ),
        P(BATCH, SEQ),
        P(),
        P(),
        P(),
        P(),
        P(None, SEQ),
        P(SEQ, None),
        P(),
        P(),
        P(),
        P(None, ("zh", "c")),
        P(("zh", "c")),
        P(("zh", "c"), None),
        P(),
    )
    return jax.shard_map(
        per_device,
        mesh=torus,
        in_specs=in_specs,
        out_specs=P(BATCH, SEQ, None),
        check_vma=False,
    )
```

```python
import math

import jax
import jax.numpy as jnp
from jax import lax
from jax.experimental import pallas as pl
from jax.experimental.pallas import tpu as pltpu
from jax.sharding import Mesh
from jax.sharding import PartitionSpec as P

AXES = ("zl", "x", "y", "zh", "c")
SEQ = ("zl", "x")
BATCH = ("y", "zh", "c")
MESH_ID = pl.DeviceIdType.MESH
TOK = 192
WIDTH = 1152
ROW = 4 * TOK
HEAD = 72
QROWS = 256
F32 = jnp.float32
BF16 = jnp.bfloat16
NT = (((1,), (1,)), ((), ()))


def norm_rows(values, gain, shift):
    center = jnp.mean(values, -1, keepdims=True)
    moved = values - center
    spread = jnp.mean(jnp.square(moved), -1, keepdims=True)
    return moved * lax.rsqrt(spread + 1e-06) * gain + shift


def line(ref):
    return ref[...].astype(F32).reshape(1, WIDTH)


def gelu(u):
    return 0.5 * u * (1.0 + jnp.tanh(math.sqrt(2.0 / math.pi) * (u + 0.044715 * u * u * u)))


def layer_kernel(
    patches,
    seg_in,
    rows_in,
    cols_in,
    rows_tab,
    cols_tab,
    ln1_gain,
    ln1_bias,
    ln2_gain,
    ln2_bias,
    out_bias,
    fc2_bias,
    fc1_bias,
    w_a,
    w_b,
    w_1,
    w_2,
    tail_1,
    tail_2,
    out,
    emb,
    nrm,
    segs,
    seg_keys,
    seg_query,
    wz,
    wp,
    wof,
    pick,
    mixed_out,
    mixed_in,
    top_own,
    sum_own,
    mix_own,
    qs,
    kv,
    own_part,
    f_own,
    f_far,
    bias_own,
    bias_far,
    stage_a,
    stage_b,
    n2,
    hid,
    mlp,
    mlp_out,
    mlp_in,
    loc_sem,
    a_send,
    a_recv,
    ay_send,
    ay_recv,
    as_send,
    as_recv,
    b_send,
    b_recv,
    bs_send,
    bs_recv,
    n_send,
    n_recv,
    s_send,
    s_recv,
    k_send,
    k_recv,
    f_send,
    f_recv,
    f1_send,
    f1_recv,
    f2_send,
    f2_recv,
    bx_send,
    bx_recv,
    r_send,
    r_recv,
    m_send,
    m_recv,
):
    zl, x, y, zh, c = (lax.axis_index(a) for a in AXES)
    z = zh * 4 + zl

    def device(dz=0, dx=0, dy=0, dc=0, mirror=False):
        zz = 7 - z if mirror else lax.rem(z + dz + 8, 8)
        return {
            "zl": lax.rem(zz, 4),
            "x": lax.rem(x + dx + 4, 4),
            "y": lax.rem(y + dy + 4, 4),
            "zh": zz // 4,
            "c": lax.rem(c + dc, 2),
        }

    def remote(src, dst, send, recv, **where):
        return pltpu.make_async_remote_copy(
            src_ref=src,
            dst_ref=dst,
            send_sem=send,
            recv_sem=recv,
            device_id=device(**where),
            device_id_type=MESH_ID,
        )

    def around(v, d):
        return lax.rem(v + d + 4, 4)

    has_prev = zl > 0
    has_next = zl < 3

    barrier = pltpu.get_barrier_semaphore()
    peers = (
        [dict(dz=d) for d in (1, -1, 2, -2)]
        + [dict(dx=d) for d in (1, -1, 2)]
        + [dict(dy=d) for d in (1, -1, 2)]
        + [dict(dc=1), dict(mirror=True)]
    )
    for peer in peers:
        pl.semaphore_signal(barrier, inc=1, device_id=device(**peer), device_id_type=MESH_ID)

    local = [
        pltpu.make_async_copy(w_a, stage_a, loc_sem.at[0]),
        pltpu.make_async_copy(w_b, stage_b, loc_sem.at[1]),
        pltpu.make_async_copy(w_1.at[0:1024], f_own.at[0:1024], loc_sem.at[2]),
        pltpu.make_async_copy(w_2.at[0:1024], f_own.at[1152:2176], loc_sem.at[3]),
    ]
    for copy in local:
        copy.start()

    local[0].wait()
    staged = stage_a[...].astype(F32)
    wz[zl] = jnp.concatenate(
        [
            staged[:HEAD],
            jnp.zeros((8, WIDTH), F32),
            staged[HEAD:],
            jnp.zeros((QROWS - 8 - 3 * HEAD, WIDTH), F32),
        ],
        axis=0,
    ).astype(BF16)
    pl.semaphore_wait(barrier, len(peers))

    def slab(buf, first, rows, send, recv, k, dz):
        ref = buf.at[zl, pl.ds(pl.multiple_of(first, 16), rows)]
        return remote(ref, ref, send.at[k], recv.at[k], dz=dz)

    eighth = (c * 4 + y) * 32
    copies_a = [
        slab(wz, eighth, 32, a_send, a_recv, 0, 1),
        slab(wz, eighth, 32, a_send, a_recv, 1, -1),
        slab(wz, eighth, 16, a_send, a_recv, 2, 2),
        slab(wz, eighth + 16, 16, a_send, a_recv, 3, -2),
    ]
    for copy in copies_a:
        copy.start()

    def wide(ref):
        return jnp.concatenate([ref[...].astype(F32), jnp.zeros((1, 64), F32)], axis=1)

    level = lax.broadcasted_iota(jnp.int32, (128, 256), 0).astype(F32)
    wanted = jnp.where(level < 64.0, wide(rows_in), wide(cols_in) + 64.0)
    hot = jnp.transpose(jnp.where(level == wanted, 1.0, 0.0))[:TOK].astype(BF16)
    tables = jnp.concatenate([rows_tab[...], cols_tab[...]], axis=0)
    embedded = patches[...].astype(F32) + jnp.dot(hot, tables, preferred_element_type=F32)
    emb[...] = embedded
    nrm[x] = norm_rows(embedded, line(ln1_gain), line(ln1_bias)).astype(BF16)
    segs[1, x] = jnp.broadcast_to(wide(seg_in), (8, 256))
    short = fc1_bias.shape[0]
    wide_bias = jnp.concatenate(
        [fc1_bias[...].astype(F32).reshape(1, short), jnp.zeros((1, WIDTH - short), F32)], axis=1
    )
    bias_own[...] = jnp.broadcast_to(wide_bias, (8, WIDTH))

    LOW, HIGH = pl.ds(0, 96), pl.ds(96, 96)
    copies_n = [
        remote(nrm.at[x], nrm.at[x], n_send.at[k], n_recv.at[k], dx=dx)
        for k, dx in enumerate((1, -1))
    ]
    copies_s = [
        remote(segs.at[1, x], segs.at[1, x], s_send.at[k], s_recv.at[k], dx=dx)
        for k, dx in enumerate((1, -1, 2))
    ]
    for copy in copies_n + copies_s:
        copy.start()

    local[1].wait()
    wof[x, pl.ds(pl.multiple_of(zl * 80, 16), 80)] = jnp.concatenate(
        [stage_b[...].astype(F32), jnp.zeros((8, WIDTH), F32)], axis=0
    ).astype(BF16)

    for copy in copies_a:
        copy.wait_recv()
    copies_ay = []
    for k, d in enumerate((-1, 1, 2)):
        for i, dy in enumerate((1, -1, 2)):
            ref = wz.at[around(zl, d), pl.ds(pl.multiple_of(eighth, 16), 32)]
            copies_ay.append(remote(ref, ref, ay_send.at[k, i], ay_recv.at[k, i], dy=dy))
    for copy in copies_ay:
        copy.start()

    def unit(py, px, first, rows):
        at = pl.multiple_of((py * 4 + px) * 144 + first, 16)
        return f_far.at[pl.ds(at, rows)]

    for copy in local[2:]:
        copy.wait()
    rest = w_1.shape[0] - 1024
    mine = pl.ds(pl.multiple_of((y * 4 + x) * 144, 16), 144)
    cross = remote(f_own.at[mine], f_far.at[mine], f_send.at[0], f_recv.at[0], mirror=True)
    cross_v = remote(bias_own, bias_far, f_send.at[1], f_recv.at[1], mirror=True)
    real = lax.broadcasted_iota(jnp.int32, (128, WIDTH), 0) < rest
    f_own[1024:1152, :] = jnp.where(real, tail_1[...], jnp.zeros((128, WIDTH), BF16))
    f_own[2176:2304, :] = jnp.where(real, tail_2[...], jnp.zeros((128, WIDTH), BF16))
    cross.start()
    cross_v.start()

    B_CUTS = ((0, 48), (48, 32))

    def rows_of(owner, core):
        first, rows = B_CUTS[core]
        return pl.ds(pl.multiple_of(owner * 80 + first, 16), rows)

    def b_copies(core):
        ref = wof.at[x, rows_of(zl, core)]
        return [
            remote(ref, ref, b_send.at[k], b_recv.at[k], dz=dz)
            for k, dz in enumerate((1, -1, (2, -2)[core]))
        ]

    def bs_copies(core):
        made = []
        for k, d in enumerate((-1, 1, 2)):
            ref = wof.at[x, rows_of(around(zl, d), core)]
            made.append(remote(ref, ref, bs_send.at[k], bs_recv.at[k], dc=1))
        return made

    def each_core(act):
        for core in (0, 1):

            @pl.when(c == core)
            def _():
                act(core)

    def start_b(core):
        for copy in b_copies(core):
            copy.start()

    def pass_b(core):
        for copy in b_copies(core):
            copy.wait_recv()
        for copy in bs_copies(core):
            copy.start()

    def take_b(core):
        for copy in bs_copies(1 - core):
            copy.wait_recv()

    def end_b(core):
        for copy in b_copies(core) + bs_copies(core):
            copy.wait_send()

    half_o = pl.ds(pl.multiple_of(c * 160, 16), 160)

    def bx_copy(k):
        ref = wof.at[x, half_o]
        return remote(ref, ref, bx_send.at[k], bx_recv.at[k], dx=(1, -1, 2)[k])

    def bxs_copy(k):
        ref = wof.at[around(x, (-1, 1, 2)[k]), half_o]
        return remote(ref, ref, bx_send.at[3 + k], bx_recv.at[3 + k], dc=1)

    each_core(start_b)

    wp[...] = jnp.zeros_like(wp)
    lane = lax.broadcasted_iota(jnp.int32, (256, 384), 1)
    line_of = lax.broadcasted_iota(jnp.int32, (256, 384), 0)
    for h in range(4):
        feature = lane - 80 * h
        chosen = (line_of - (16 * h + HEAD) == feature) & (feature >= 0) & (feature < HEAD)
        pick[h] = jnp.where(chosen, 1.0, 0.0).astype(BF16)

    @pl.when(jnp.logical_not(has_prev))
    def _():
        kv[0:ROW, :] = jnp.zeros((ROW, 640), BF16)
        segs[0] = jnp.full((4, 8, 256), -1.0, F32)

    @pl.when(jnp.logical_not(has_next))
    def _():
        kv[ROW : 2 * ROW, :] = jnp.zeros((ROW, 640), BF16)
        segs[2] = jnp.full((4, 8, 256), -1.0, F32)

    left, right, far_x = around(x, -1), around(x, 1), around(x, 2)
    copies_n[0].wait_recv()
    on_right = remote(nrm.at[left, LOW], nrm.at[left, LOW], n_send.at[2], n_recv.at[2], dx=1)
    on_right.start()
    copies_n[1].wait_recv()
    on_left = remote(nrm.at[right, HIGH], nrm.at[right, HIGH], n_send.at[3], n_recv.at[3], dx=-1)
    on_left.start()

    def to_sibling(buf, first, rows, send, recv):
        at = pl.ds(pl.multiple_of(first, 16), rows)
        made = []
        for k, d in enumerate((-1, 1, 2)):
            ref = buf.at[around(zl, d), at]
            made.append(remote(ref, ref, send.at[k], recv.at[k], dc=1))
        return made

    copies_as = to_sibling(wz, c * (QROWS // 2), QROWS // 2, as_send, as_recv)
    for copy in copies_ay:
        copy.wait_recv()
    for copy in copies_as:
        copy.start()
    for copy in copies_as:
        copy.wait_recv()
    for h in range(4):
        wp[144 * h : 144 * h + 80, :] = wz[h, 0:80, :]
        wp[512 + 144 * h : 656 + 144 * h, :] = wz[h, 80:224, :]

    copies_k = []

    def project(k, source):
        tokens = nrm[source]
        at = pl.ds(pl.multiple_of(source * TOK, TOK), TOK)
        here = pl.ds(pl.multiple_of(2 * ROW + source * TOK, TOK), TOK)
        as_next = pl.ds(pl.multiple_of(ROW + source * TOK, TOK), TOK)
        kv[here, :] = lax.dot_general(
            tokens, wp[512:1152, :], NT, preferred_element_type=F32
        ).astype(BF16)
        up = remote(kv.at[here], kv.at[at], k_send.at[0, k], k_recv.at[0, k], dz=1)
        down = remote(kv.at[here], kv.at[as_next], k_send.at[1, k], k_recv.at[1, k], dz=-1)
        copies_k.append((up, down))
        pl.when(has_next)(up.start)
        pl.when(has_prev)(down.start)
        qs[at, :] = lax.dot_general(
            tokens, wp[0:512, :], NT, preferred_element_type=F32
        ).astype(BF16)

    project(0, x)
    project(1, left)
    project(2, right)

    PARTS = ((0, 96, 48), (96, 48, 32))
    def held(part, k, db=0):
        d = (0, -1, 1, 2)[k]
        if part == 0:
            return around(y, db), around(x, d)
        return around(y, d), around(x, db)

    def along(part, phase, d):
        return dict(dx=d) if (part == 0) == (phase == 0) else dict(dy=d)

    def first_copy(part, i):
        first, rows, _ = PARTS[part]
        ref = unit(y, x, first, rows)
        d = (1, -1, 2)[i]
        return remote(ref, ref, f1_send.at[part, i], f1_recv.at[part, i], **along(part, 0, d))

    def second_copy(part, k, i):
        first, rows, _ = PARTS[part]
        ref = unit(*held(part, k), first, rows)
        return remote(
            ref, ref, f2_send.at[part, k, i], f2_recv.at[part, k, i], **along(part, 1, (1, -1)[i])
        )

    def hand_copy(part, k, i):
        first, rows, half = PARTS[part]
        cut = ((first, half), (first + half, rows - half))[i]
        d = (1, -1)[i]
        ref = unit(*held(part, k, -d), *cut)
        at = (part, k, 2 + i)
        return remote(ref, ref, f2_send.at[at], f2_recv.at[at], **along(part, 1, d))

    def start_first(part):
        for i in range(3):
            first_copy(part, i).start()

    def start_second(part, k):
        for i in range(2):
            second_copy(part, k, i).start()

    def hand_on(part, k):
        for i in range(2):
            second_copy(part, k, i).wait_recv()
            hand_copy(part, k, i).start()

    on_right.wait_recv()
    on_left.wait_recv()
    project(3, far_x)
    each_core(pass_b)
    each_core(take_b)
    for k in range(3):
        bx_copy(k).start()
    cross.wait_recv()
    for part in (0, 1):
        start_first(part)
        start_second(part, 0)
    for copy in copies_s:
        copy.wait_recv()
    seg_up = remote(segs.at[1], segs.at[0], s_send.at[3], s_recv.at[3], dz=1)
    seg_down = remote(segs.at[1], segs.at[2], s_send.at[4], s_recv.at[4], dz=-1)
    pl.when(has_next)(seg_up.start)
    pl.when(has_prev)(seg_down.start)


    scale = 1.0 / math.sqrt(HEAD)
    seg_keys[0] = jnp.concatenate([segs[1, b][:, :TOK] for b in range(4)] + [segs[1, 0][:, :TOK]], axis=1)
    for j in range(4):
        spread = jnp.concatenate([segs[1, j]] * 16, axis=0)
        seg_query[j] = jnp.transpose(spread)[:TOK]

    def scores_of(j, h, keys):
        at = pl.ds(pl.multiple_of(j * TOK, TOK), TOK)
        return lax.dot_general(
            qs[at, 128 * h : 128 * h + 128],
            kv[keys, 128 * h : 128 * h + 128],
            NT,
            preferred_element_type=F32,
        )

    def attend_own(j):
        same = seg_query[j][:, 0:1] == seg_keys[0][0:1, :ROW]
        own = pl.ds(2 * ROW, ROW)
        for h in range(4):
            scores = jnp.where(same, scores_of(j, h, own), -jnp.inf)
            top = jnp.max(scores, -1, keepdims=True)
            expo = jnp.exp((scores - top) * scale)
            top_own[j, h] = jnp.broadcast_to(top, (TOK, 128))
            sum_own[j, h] = jnp.broadcast_to(jnp.sum(expo, -1, keepdims=True), (TOK, 128))
            mix_own[j, h] = jnp.dot(
                expo.astype(BF16), kv[own, 128 * h : 128 * h + 256], preferred_element_type=F32
            )

    def own_steps(first):
        def step(j, carry):
            attend_own(j)
            return carry

        lax.fori_loop(first, first + 2, step, 0)

    own_steps(0)
    for k in (1, 2, 3):
        for part in (1, 0):
            first_copy(part, k - 1).wait_recv()
            start_second(part, k)
    own_steps(2)
    for part in (1, 0):
        hand_on(part, 0)

    pl.when(has_prev)(seg_up.wait_recv)
    pl.when(has_next)(seg_down.wait_recv)
    around_segs = [segs[r, b][:, :TOK] for r in (0, 2) for b in range(4)]
    for j in range(4):
        seg_keys[j] = jnp.concatenate(around_segs[j : j + 5], axis=1)
    for up, down in copies_k:
        pl.when(has_prev)(up.wait_recv)
        pl.when(has_next)(down.wait_recv)

    def attend(j):
        window = pl.ds(pl.multiple_of(j * TOK, TOK), 5 * TOK)
        same = seg_query[j][:, 0:1] == seg_keys[j][0:1, :]
        total = None
        for h in range(4):
            scores = jnp.where(same, scores_of(j, h, window), -jnp.inf)
            before = top_own[j, h][:, 0:1]
            top = jnp.maximum(jnp.max(scores, -1, keepdims=True), before)
            expo = jnp.exp((scores - top) * scale)
            kept = jnp.exp((before - top) * scale)
            weight = jnp.sum(expo, -1, keepdims=True) + kept * sum_own[j, h][:, 0:1]
            mixed = jnp.dot(
                expo.astype(BF16), kv[window, 128 * h : 128 * h + 256], preferred_element_type=F32
            )
            mixed = ((mixed + kept * mix_own[j, h]) / weight).astype(BF16)
            term = jnp.dot(mixed, pick[h], preferred_element_type=F32)
            total = term if total is None else total + term
        return total.astype(BF16)

    def mixed_copy(k):
        return remote(
            mixed_out.at[k], mixed_in.at[k], r_send.at[k], r_recv.at[k], dx=(2, 1, -1)[k]
        )

    def attend_step(k, carry):
        d = jnp.where(k == 0, 2, jnp.where(k == 1, 1, jnp.where(k == 2, 3, 0)))
        got = attend(around(x, d))
        mixed_out[k] = got
        for step in range(3):

            @pl.when(k == step)
            def _():
                mixed_copy(step).start()
                for part in (1, 0):
                    hand_on(part, step + 1)
                bx_copy(step).wait_recv()
                bxs_copy(step).start()

        return carry

    lax.fori_loop(0, 4, attend_step, 0)

    def projected(held_in, px):
        return jnp.dot(held_in[:, 0:320], wof[px], preferred_element_type=F32)

    attended = emb[...] + projected(mixed_out[3], x) + line(out_bias)
    for k in range(3):
        bxs_copy(k).wait_recv()
    for k, d in enumerate((2, -1, 1)):
        mixed_copy(k).wait_recv()
        attended = attended + projected(mixed_in[k], around(x, d))
    own_part[...] = attended
    n2[c] = norm_rows(attended, line(ln2_gain), line(ln2_bias)).astype(BF16)
    give = remote(n2.at[c], n2.at[c], m_send.at[0], m_recv.at[0], dc=1)
    give.start()
    give.wait_recv()

    tokens = n2[...].reshape(2 * TOK, WIDTH)

    def hidden_of(weights, biases):
        def step(i, carry):
            at = pl.ds(pl.multiple_of(i * 384, 384), 384)
            inner = lax.dot_general(tokens, weights[at, :], NT, preferred_element_type=F32)
            hid[:, at] = gelu(inner + biases[0:1, at]).astype(BF16)
            return carry

        lax.fori_loop(0, 3, step, 0, unroll=True)

    def project_hidden(weights, first):
        def step(i, carry):
            at = pl.ds(pl.multiple_of(i * 384, 384), 384)
            got = jnp.dot(hid[...], weights[WIDTH : 2 * WIDTH, at], preferred_element_type=F32)
            mlp[:, at] = got if first else mlp[:, at] + got
            return carry

        lax.fori_loop(0, 3, step, 0, unroll=True)

    hidden_of(f_own, bias_own)
    project_hidden(f_own, True)
    for part in (0, 1):
        for k in range(4):
            for i in range(2):
                hand_copy(part, k, i).wait_recv()
    cross_v.wait_recv()
    hidden_of(f_far, bias_far)
    project_hidden(f_far, False)

    mine_at = pl.ds(pl.multiple_of(c * TOK, TOK), TOK)
    other_at = pl.ds(pl.multiple_of((1 - c) * TOK, TOK), TOK)
    mlp_out[...] = mlp[other_at, :].astype(BF16)
    back = remote(mlp_out, mlp_in, m_send.at[1], m_recv.at[1], dc=1)
    back.start()
    mine_sum = own_part[...] + line(fc2_bias) + mlp[mine_at, :]
    back.wait_recv()
    out[...] = (mine_sum + mlp_in[...].astype(F32)).astype(BF16)

    for copy in copies_a + copies_ay + copies_as + copies_n + copies_s:
        copy.wait_send()
    for up, down in copies_k:
        pl.when(has_next)(up.wait_send)
        pl.when(has_prev)(down.wait_send)
    pl.when(has_next)(seg_up.wait_send)
    pl.when(has_prev)(seg_down.wait_send)
    for copy in [cross, cross_v, give, back, on_right, on_left]:
        copy.wait_send()
    each_core(end_b)
    for k in range(3):
        bx_copy(k).wait_send()
        bxs_copy(k).wait_send()
        mixed_copy(k).wait_send()
    for part in (0, 1):
        for i in range(3):
            first_copy(part, i).wait_send()
        for k in range(4):
            for i in range(2):
                second_copy(part, k, i).wait_send()
                hand_copy(part, k, i).wait_send()


def layer_call(*operands):
    vmem = pl.BlockSpec(memory_space=pltpu.VMEM)
    hbm = pl.BlockSpec(memory_space=pl.ANY)
    edge = pl.BlockSpec((128, WIDTH), lambda i: (8, 0))
    dma = pltpu.SemaphoreType.DMA
    scratch = [
        pltpu.VMEM((TOK, WIDTH), F32),
        pltpu.VMEM((4, TOK, WIDTH), BF16),
        pltpu.VMEM((3, 4, 8, 256), F32),
        pltpu.VMEM((4, 8, 5 * TOK), F32),
        pltpu.VMEM((4, TOK, 128), F32),
        pltpu.VMEM((4, QROWS, WIDTH), BF16),
        pltpu.VMEM((WIDTH, WIDTH), BF16),
        pltpu.VMEM((4, 320, WIDTH), BF16),
        pltpu.VMEM((4, 256, 384), BF16),
        pltpu.VMEM((4, TOK, 384), BF16),
        pltpu.VMEM((3, TOK, 384), BF16),
        pltpu.VMEM((4, 4, TOK, 128), F32),
        pltpu.VMEM((4, 4, TOK, 128), F32),
        pltpu.VMEM((4, 4, TOK, 256), F32),
        pltpu.VMEM((ROW, 512), BF16),
        pltpu.VMEM((3 * ROW, 640), BF16),
        pltpu.VMEM((TOK, WIDTH), F32),
        pltpu.VMEM((2 * WIDTH, WIDTH), BF16),
        pltpu.VMEM((2 * WIDTH, WIDTH), BF16),
        pltpu.VMEM((8, WIDTH), F32),
        pltpu.VMEM((8, WIDTH), F32),
        pltpu.VMEM((3 * HEAD, WIDTH), BF16),
        pltpu.VMEM((HEAD, WIDTH), BF16),
        pltpu.VMEM((2, TOK, WIDTH), BF16),
        pltpu.VMEM((2 * TOK, WIDTH), BF16),
        pltpu.VMEM((2 * TOK, WIDTH), F32),
        pltpu.VMEM((TOK, WIDTH), BF16),
        pltpu.VMEM((TOK, WIDTH), BF16),
        dma((4,)),
    ]
    for shape in ((4,), (3, 3), (3,), (4,), (3,), (4,), (5,), (2, 4), (2,), (2, 3), (2, 4, 4), (6,), (3,), (2,)):
        scratch += [dma(shape), dma(shape)]
    return pl.pallas_call(
        layer_kernel,
        out_shape=jax.ShapeDtypeStruct((TOK, WIDTH), BF16),
        grid=(1,),
        in_specs=[vmem] * 13 + [hbm] * 4 + [edge] * 2,
        out_specs=vmem,
        scratch_shapes=scratch,
        compiler_params=pltpu.CompilerParams(
            collective_id=0, has_side_effects=True, vmem_limit_bytes=60 << 20
        ),
        name="encoder_layer",
    )(*operands)


def per_device(
    patches,
    seg_ids,
    pos_rows,
    pos_cols,
    row_table,
    col_table,
    ln1_gain,
    ln1_bias,
    w_qkv,
    w_out,
    out_bias,
    ln2_gain,
    ln2_bias,
    w_fc1,
    fc1_bias,
    w_fc2,
    fc2_bias,
):
    w_1 = w_fc1.T
    return layer_call(
        patches[0],
        seg_ids,
        pos_rows,
        pos_cols,
        row_table,
        col_table,
        ln1_gain,
        ln1_bias,
        ln2_gain,
        ln2_bias,
        out_bias,
        fc2_bias,
        fc1_bias,
        w_qkv.T,
        w_out,
        w_1,
        w_fc2,
        w_1,
        w_fc2,
    )[None]


def solution(mesh):
    torus = Mesh(mesh.devices.reshape(4, 4, 4, 2, 2), AXES)
    in_specs = (
        P(BATCH, SEQ, None),
        P(BATCH, SEQ),
        P(BATCH, SEQ),
        P(BATCH, SEQ),
        P(),
        P(),
        P(),
        P(),
        P(None, SEQ),
        P(SEQ, None),
        P(),
        P(),
        P(),
        P(None, ("zh", "c")),
        P(("zh", "c")),
        P(("zh", "c"), None),
        P(),
    )
    return jax.shard_map(
        per_device,
        mesh=torus,
        in_specs=in_specs,
        out_specs=P(BATCH, SEQ, None),
        check_vma=False,
    )
```

```python
import math

import jax
import jax.numpy as jnp
from jax import lax
from jax.experimental import pallas as pl
from jax.experimental.pallas import tpu as pltpu
from jax.sharding import Mesh
from jax.sharding import PartitionSpec as P

AXES = ("zl", "x", "y", "zh", "c")
SEQ = ("zl", "x")
BATCH = ("y", "zh", "c")
MESH_ID = pl.DeviceIdType.MESH
TOK = 192
WIDTH = 1152
ROW = 4 * TOK
HEAD = 72
QROWS = 256
F32 = jnp.float32
BF16 = jnp.bfloat16
NT = (((1,), (1,)), ((), ()))


def norm_rows(values, gain, shift):
    center = jnp.mean(values, -1, keepdims=True)
    moved = values - center
    spread = jnp.mean(jnp.square(moved), -1, keepdims=True)
    return moved * lax.rsqrt(spread + 1e-06) * gain + shift


def line(ref):
    return ref[...].astype(F32).reshape(1, WIDTH)


def gelu(u):
    return 0.5 * u * (1.0 + jnp.tanh(math.sqrt(2.0 / math.pi) * (u + 0.044715 * u * u * u)))


def layer_kernel(
    patches,
    seg_in,
    rows_in,
    cols_in,
    rows_tab,
    cols_tab,
    ln1_gain,
    ln1_bias,
    ln2_gain,
    ln2_bias,
    out_bias,
    fc2_bias,
    fc1_bias,
    w_a,
    w_b,
    w_1,
    w_2,
    tail_1,
    tail_2,
    out,
    emb,
    nrm,
    segs,
    seg_keys,
    seg_query,
    wz,
    wp,
    wof,
    pick,
    mixed_out,
    mixed_in,
    top_own,
    sum_own,
    mix_own,
    qs,
    kv,
    own_part,
    f_own,
    f_far,
    bias_own,
    bias_far,
    stage_a,
    stage_b,
    n2,
    hid,
    mlp,
    mlp_out,
    mlp_in,
    loc_sem,
    a_send,
    a_recv,
    ay_send,
    ay_recv,
    as_send,
    as_recv,
    b_send,
    b_recv,
    bs_send,
    bs_recv,
    n_send,
    n_recv,
    s_send,
    s_recv,
    k_send,
    k_recv,
    f_send,
    f_recv,
    f1_send,
    f1_recv,
    f2_send,
    f2_recv,
    bx_send,
    bx_recv,
    r_send,
    r_recv,
    m_send,
    m_recv,
):
    zl, x, y, zh, c = (lax.axis_index(a) for a in AXES)
    z = zh * 4 + zl

    def device(dz=0, dx=0, dy=0, dc=0, mirror=False):
        zz = 7 - z if mirror else lax.rem(z + dz + 8, 8)
        return {
            "zl": lax.rem(zz, 4),
            "x": lax.rem(x + dx + 4, 4),
            "y": lax.rem(y + dy + 4, 4),
            "zh": zz // 4,
            "c": lax.rem(c + dc, 2),
        }

    def remote(src, dst, send, recv, **where):
        return pltpu.make_async_remote_copy(
            src_ref=src,
            dst_ref=dst,
            send_sem=send,
            recv_sem=recv,
            device_id=device(**where),
            device_id_type=MESH_ID,
        )

    def around(v, d):
        return lax.rem(v + d + 4, 4)

    has_prev = zl > 0
    has_next = zl < 3

    barrier = pltpu.get_barrier_semaphore()
    peers = (
        [dict(dz=d) for d in (1, -1, 2, -2)]
        + [dict(dx=d) for d in (1, -1, 2)]
        + [dict(dy=d) for d in (1, -1, 2)]
        + [dict(dc=1), dict(mirror=True)]
    )
    for peer in peers:
        pl.semaphore_signal(barrier, inc=1, device_id=device(**peer), device_id_type=MESH_ID)

    local = [
        pltpu.make_async_copy(w_a, stage_a, loc_sem.at[0]),
        pltpu.make_async_copy(w_b, stage_b, loc_sem.at[1]),
        pltpu.make_async_copy(w_1.at[0:1024], f_own.at[0:1024], loc_sem.at[2]),
        pltpu.make_async_copy(w_2.at[0:1024], f_own.at[1152:2176], loc_sem.at[3]),
    ]
    for copy in local:
        copy.start()

    local[0].wait()
    staged = stage_a[...].astype(F32)
    wz[zl] = jnp.concatenate(
        [
            staged[:HEAD],
            jnp.zeros((8, WIDTH), F32),
            staged[HEAD:],
            jnp.zeros((QROWS - 8 - 3 * HEAD, WIDTH), F32),
        ],
        axis=0,
    ).astype(BF16)
    pl.semaphore_wait(barrier, len(peers))

    def slab(buf, first, rows, send, recv, k, dz):
        ref = buf.at[zl, pl.ds(pl.multiple_of(first, 16), rows)]
        return remote(ref, ref, send.at[k], recv.at[k], dz=dz)

    eighth = (c * 4 + y) * 32
    copies_a = [
        slab(wz, eighth, 32, a_send, a_recv, 0, 1),
        slab(wz, eighth, 32, a_send, a_recv, 1, -1),
        slab(wz, eighth, 16, a_send, a_recv, 2, 2),
        slab(wz, eighth + 16, 16, a_send, a_recv, 3, -2),
    ]
    for copy in copies_a:
        copy.start()

    def wide(ref):
        return jnp.concatenate([ref[...].astype(F32), jnp.zeros((1, 64), F32)], axis=1)

    level = lax.broadcasted_iota(jnp.int32, (128, 256), 0).astype(F32)
    wanted = jnp.where(level < 64.0, wide(rows_in), wide(cols_in) + 64.0)
    hot = jnp.transpose(jnp.where(level == wanted, 1.0, 0.0))[:TOK].astype(BF16)
    tables = jnp.concatenate([rows_tab[...], cols_tab[...]], axis=0)
    embedded = patches[...].astype(F32) + jnp.dot(hot, tables, preferred_element_type=F32)
    emb[...] = embedded
    nrm[x] = norm_rows(embedded, line(ln1_gain), line(ln1_bias)).astype(BF16)
    segs[1, x] = jnp.broadcast_to(wide(seg_in), (8, 256))
    short = fc1_bias.shape[0]
    wide_bias = jnp.concatenate(
        [fc1_bias[...].astype(F32).reshape(1, short), jnp.zeros((1, WIDTH - short), F32)], axis=1
    )
    bias_own[...] = jnp.broadcast_to(wide_bias, (8, WIDTH))

    LOW, HIGH = pl.ds(0, 96), pl.ds(96, 96)
    copies_n = [
        remote(nrm.at[x], nrm.at[x], n_send.at[k], n_recv.at[k], dx=dx)
        for k, dx in enumerate((1, -1))
    ]
    copies_s = [
        remote(segs.at[1, x], segs.at[1, x], s_send.at[k], s_recv.at[k], dx=dx)
        for k, dx in enumerate((1, -1, 2))
    ]
    for copy in copies_n + copies_s:
        copy.start()

    local[1].wait()
    wof[x, pl.ds(pl.multiple_of(zl * 80, 16), 80)] = jnp.concatenate(
        [stage_b[...].astype(F32), jnp.zeros((8, WIDTH), F32)], axis=0
    ).astype(BF16)

    for copy in copies_a:
        copy.wait_recv()
    copies_ay = []
    for k, d in enumerate((-1, 1, 2)):
        for i, dy in enumerate((1, -1, 2)):
            ref = wz.at[around(zl, d), pl.ds(pl.multiple_of(eighth, 16), 32)]
            copies_ay.append(remote(ref, ref, ay_send.at[k, i], ay_recv.at[k, i], dy=dy))
    for copy in copies_ay:
        copy.start()

    def unit(py, px, first, rows):
        at = pl.multiple_of((py * 4 + px) * 144 + first, 16)
        return f_far.at[pl.ds(at, rows)]

    for copy in local[2:]:
        copy.wait()
    rest = w_1.shape[0] - 1024
    mine = pl.ds(pl.multiple_of((y * 4 + x) * 144, 16), 144)
    cross = remote(f_own.at[mine], f_far.at[mine], f_send.at[0], f_recv.at[0], mirror=True)
    cross_v = remote(bias_own, bias_far, f_send.at[1], f_recv.at[1], mirror=True)
    real = lax.broadcasted_iota(jnp.int32, (128, WIDTH), 0) < rest
    f_own[1024:1152, :] = jnp.where(real, tail_1[...], jnp.zeros((128, WIDTH), BF16))
    f_own[2176:2304, :] = jnp.where(real, tail_2[...], jnp.zeros((128, WIDTH), BF16))
    cross.start()
    cross_v.start()

    B_CUTS = ((0, 48), (48, 32))

    def rows_of(owner, core):
        first, rows = B_CUTS[core]
        return pl.ds(pl.multiple_of(owner * 80 + first, 16), rows)

    def b_copies(core):
        ref = wof.at[x, rows_of(zl, core)]
        return [
            remote(ref, ref, b_send.at[k], b_recv.at[k], dz=dz)
            for k, dz in enumerate((1, -1, (2, -2)[core]))
        ]

    def bs_copies(core):
        made = []
        for k, d in enumerate((-1, 1, 2)):
            ref = wof.at[x, rows_of(around(zl, d), core)]
            made.append(remote(ref, ref, bs_send.at[k], bs_recv.at[k], dc=1))
        return made

    def each_core(act):
        for core in (0, 1):

            @pl.when(c == core)
            def _():
                act(core)

    def start_b(core):
        for copy in b_copies(core):
            copy.start()

    def pass_b(core):
        for copy in b_copies(core):
            copy.wait_recv()
        for copy in bs_copies(core):
            copy.start()

    def take_b(core):
        for copy in bs_copies(1 - core):
            copy.wait_recv()

    def end_b(core):
        for copy in b_copies(core) + bs_copies(core):
            copy.wait_send()

    half_o = pl.ds(pl.multiple_of(c * 160, 16), 160)

    def bx_copy(k):
        ref = wof.at[x, half_o]
        return remote(ref, ref, bx_send.at[k], bx_recv.at[k], dx=(1, -1, 2)[k])

    def bxs_copy(k):
        ref = wof.at[around(x, (-1, 1, 2)[k]), half_o]
        return remote(ref, ref, bx_send.at[3 + k], bx_recv.at[3 + k], dc=1)

    each_core(start_b)

    wp[...] = jnp.zeros_like(wp)
    lane = lax.broadcasted_iota(jnp.int32, (256, 384), 1)
    line_of = lax.broadcasted_iota(jnp.int32, (256, 384), 0)
    for h in range(4):
        feature = lane - 80 * h
        chosen = (line_of - (16 * h + HEAD) == feature) & (feature >= 0) & (feature < HEAD)
        pick[h] = jnp.where(chosen, 1.0, 0.0).astype(BF16)

    @pl.when(jnp.logical_not(has_prev))
    def _():
        kv[0:ROW, :] = jnp.zeros((ROW, 640), BF16)
        segs[0] = jnp.full((4, 8, 256), -1.0, F32)

    @pl.when(jnp.logical_not(has_next))
    def _():
        kv[ROW : 2 * ROW, :] = jnp.zeros((ROW, 640), BF16)
        segs[2] = jnp.full((4, 8, 256), -1.0, F32)

    left, right, far_x = around(x, -1), around(x, 1), around(x, 2)
    copies_n[0].wait_recv()
    on_right = remote(nrm.at[left, LOW], nrm.at[left, LOW], n_send.at[2], n_recv.at[2], dx=1)
    on_right.start()
    copies_n[1].wait_recv()
    on_left = remote(nrm.at[right, HIGH], nrm.at[right, HIGH], n_send.at[3], n_recv.at[3], dx=-1)
    on_left.start()

    def to_sibling(buf, first, rows, send, recv):
        at = pl.ds(pl.multiple_of(first, 16), rows)
        made = []
        for k, d in enumerate((-1, 1, 2)):
            ref = buf.at[around(zl, d), at]
            made.append(remote(ref, ref, send.at[k], recv.at[k], dc=1))
        return made

    copies_as = to_sibling(wz, c * (QROWS // 2), QROWS // 2, as_send, as_recv)
    for copy in copies_ay:
        copy.wait_recv()
    for copy in copies_as:
        copy.start()
    for copy in copies_as:
        copy.wait_recv()
    for h in range(4):
        wp[144 * h : 144 * h + 80, :] = wz[h, 0:80, :]
        wp[512 + 144 * h : 656 + 144 * h, :] = wz[h, 80:224, :]

    copies_k = []

    def project(k, source):
        tokens = nrm[source]
        at = pl.ds(pl.multiple_of(source * TOK, TOK), TOK)
        here = pl.ds(pl.multiple_of(2 * ROW + source * TOK, TOK), TOK)
        as_next = pl.ds(pl.multiple_of(ROW + source * TOK, TOK), TOK)
        kv[here, :] = lax.dot_general(
            tokens, wp[512:1152, :], NT, preferred_element_type=F32
        ).astype(BF16)
        up = remote(kv.at[here], kv.at[at], k_send.at[0, k], k_recv.at[0, k], dz=1)
        down = remote(kv.at[here], kv.at[as_next], k_send.at[1, k], k_recv.at[1, k], dz=-1)
        copies_k.append((up, down))
        pl.when(has_next)(up.start)
        pl.when(has_prev)(down.start)
        qs[at, :] = lax.dot_general(
            tokens, wp[0:512, :], NT, preferred_element_type=F32
        ).astype(BF16)

    PARTS = ((0, 112, 64), (112, 32, 16))
    def held(part, k, db=0):
        d = (0, -1, 1, 2)[k]
        if part == 0:
            return around(y, db), around(x, d)
        return around(y, d), around(x, db)

    def along(part, phase, d):
        return dict(dx=d) if (part == 0) == (phase == 0) else dict(dy=d)

    def first_copy(part, i):
        first, rows, _ = PARTS[part]
        ref = unit(y, x, first, rows)
        d = (1, -1, 2)[i]
        return remote(ref, ref, f1_send.at[part, i], f1_recv.at[part, i], **along(part, 0, d))

    def second_copy(part, k, i):
        first, rows, _ = PARTS[part]
        ref = unit(*held(part, k), first, rows)
        return remote(
            ref, ref, f2_send.at[part, k, i], f2_recv.at[part, k, i], **along(part, 1, (1, -1)[i])
        )

    def hand_copy(part, k, i):
        first, rows, half = PARTS[part]
        cut = ((first, half), (first + half, rows - half))[i]
        d = (1, -1)[i]
        ref = unit(*held(part, k, -d), *cut)
        at = (part, k, 2 + i)
        return remote(ref, ref, f2_send.at[at], f2_recv.at[at], **along(part, 1, d))

    def start_first(part):
        for i in range(3):
            first_copy(part, i).start()

    def start_second(part, k):
        for i in range(2):
            second_copy(part, k, i).start()

    def hand_on(part, k):
        for i in range(2):
            second_copy(part, k, i).wait_recv()
            hand_copy(part, k, i).start()

    project(0, x)
    cross.wait_recv()
    for part in (0, 1):
        start_first(part)
        start_second(part, 0)
    project(1, left)
    project(2, right)

    on_right.wait_recv()
    on_left.wait_recv()
    project(3, far_x)
    each_core(pass_b)
    each_core(take_b)
    for copy in copies_s:
        copy.wait_recv()
    seg_up = remote(segs.at[1], segs.at[0], s_send.at[3], s_recv.at[3], dz=1)
    seg_down = remote(segs.at[1], segs.at[2], s_send.at[4], s_recv.at[4], dz=-1)
    pl.when(has_next)(seg_up.start)
    pl.when(has_prev)(seg_down.start)


    scale = 1.0 / math.sqrt(HEAD)
    seg_keys[0] = jnp.concatenate([segs[1, b][:, :TOK] for b in range(4)] + [segs[1, 0][:, :TOK]], axis=1)
    for j in range(4):
        spread = jnp.concatenate([segs[1, j]] * 16, axis=0)
        seg_query[j] = jnp.transpose(spread)[:TOK]

    def scores_of(j, h, keys):
        at = pl.ds(pl.multiple_of(j * TOK, TOK), TOK)
        return lax.dot_general(
            qs[at, 128 * h : 128 * h + 128],
            kv[keys, 128 * h : 128 * h + 128],
            NT,
            preferred_element_type=F32,
        )

    def attend_own(j):
        same = seg_query[j][:, 0:1] == seg_keys[0][0:1, :ROW]
        own = pl.ds(2 * ROW, ROW)
        for h in range(4):
            scores = jnp.where(same, scores_of(j, h, own), -jnp.inf)
            top = jnp.max(scores, -1, keepdims=True)
            expo = jnp.exp((scores - top) * scale)
            top_own[j, h] = jnp.broadcast_to(top, (TOK, 128))
            sum_own[j, h] = jnp.broadcast_to(jnp.sum(expo, -1, keepdims=True), (TOK, 128))
            mix_own[j, h] = jnp.dot(
                expo.astype(BF16), kv[own, 128 * h : 128 * h + 256], preferred_element_type=F32
            )

    def own_steps(first):
        def step(j, carry):
            attend_own(j)
            return carry

        lax.fori_loop(first, first + 2, step, 0)

    for k in (1, 2, 3):
        for part in (1, 0):
            first_copy(part, k - 1).wait_recv()
            start_second(part, k)
    for k in range(3):
        bx_copy(k).start()
    own_steps(0)
    for part in (1, 0):
        hand_on(part, 0)
    own_steps(2)
    for part in (1, 0):
        hand_on(part, 1)

    pl.when(has_prev)(seg_up.wait_recv)
    pl.when(has_next)(seg_down.wait_recv)
    around_segs = [segs[r, b][:, :TOK] for r in (0, 2) for b in range(4)]
    for j in range(4):
        seg_keys[j] = jnp.concatenate(around_segs[j : j + 5], axis=1)
    for up, down in copies_k:
        pl.when(has_prev)(up.wait_recv)
        pl.when(has_next)(down.wait_recv)

    def attend(j):
        window = pl.ds(pl.multiple_of(j * TOK, TOK), 5 * TOK)
        same = seg_query[j][:, 0:1] == seg_keys[j][0:1, :]
        total = None
        for h in range(4):
            scores = jnp.where(same, scores_of(j, h, window), -jnp.inf)
            before = top_own[j, h][:, 0:1]
            top = jnp.maximum(jnp.max(scores, -1, keepdims=True), before)
            expo = jnp.exp((scores - top) * scale)
            kept = jnp.exp((before - top) * scale)
            weight = jnp.sum(expo, -1, keepdims=True) + kept * sum_own[j, h][:, 0:1]
            mixed = jnp.dot(
                expo.astype(BF16), kv[window, 128 * h : 128 * h + 256], preferred_element_type=F32
            )
            mixed = ((mixed + kept * mix_own[j, h]) / weight).astype(BF16)
            term = jnp.dot(mixed, pick[h], preferred_element_type=F32)
            total = term if total is None else total + term
        return total.astype(BF16)

    def mixed_copy(k):
        return remote(
            mixed_out.at[k], mixed_in.at[k], r_send.at[k], r_recv.at[k], dx=(2, 1, -1)[k]
        )

    def attend_step(k, carry):
        d = jnp.where(k == 0, 2, jnp.where(k == 1, 1, jnp.where(k == 2, 3, 0)))
        got = attend(around(x, d))
        mixed_out[k] = got
        for step in range(3):

            @pl.when(k == step)
            def _():
                mixed_copy(step).start()
                if step < 2:
                    for part in (1, 0):
                        hand_on(part, step + 2)
                bx_copy(step).wait_recv()
                bxs_copy(step).start()

        return carry

    lax.fori_loop(0, 4, attend_step, 0)

    def projected(held_in, px):
        return jnp.dot(held_in[:, 0:320], wof[px], preferred_element_type=F32)

    attended = emb[...] + projected(mixed_out[3], x) + line(out_bias)
    for k in range(3):
        bxs_copy(k).wait_recv()
    for k, d in enumerate((2, -1, 1)):
        mixed_copy(k).wait_recv()
        attended = attended + projected(mixed_in[k], around(x, d))
    own_part[...] = attended
    n2[c] = norm_rows(attended, line(ln2_gain), line(ln2_bias)).astype(BF16)
    give = remote(n2.at[c], n2.at[c], m_send.at[0], m_recv.at[0], dc=1)
    give.start()
    give.wait_recv()

    tokens = n2[...].reshape(2 * TOK, WIDTH)

    def hidden_of(weights, biases):
        def step(i, carry):
            at = pl.ds(pl.multiple_of(i * 384, 384), 384)
            inner = lax.dot_general(tokens, weights[at, :], NT, preferred_element_type=F32)
            hid[:, at] = gelu(inner + biases[0:1, at]).astype(BF16)
            return carry

        lax.fori_loop(0, 3, step, 0, unroll=True)

    def project_hidden(weights, first):
        def step(i, carry):
            at = pl.ds(pl.multiple_of(i * 384, 384), 384)
            got = jnp.dot(hid[...], weights[WIDTH : 2 * WIDTH, at], preferred_element_type=F32)
            mlp[:, at] = got if first else mlp[:, at] + got
            return carry

        lax.fori_loop(0, 3, step, 0, unroll=True)

    hidden_of(f_own, bias_own)
    project_hidden(f_own, True)
    for part in (0, 1):
        for k in range(4):
            for i in range(2):
                hand_copy(part, k, i).wait_recv()
    cross_v.wait_recv()
    hidden_of(f_far, bias_far)
    project_hidden(f_far, False)

    mine_at = pl.ds(pl.multiple_of(c * TOK, TOK), TOK)
    other_at = pl.ds(pl.multiple_of((1 - c) * TOK, TOK), TOK)
    mlp_out[...] = mlp[other_at, :].astype(BF16)
    back = remote(mlp_out, mlp_in, m_send.at[1], m_recv.at[1], dc=1)
    back.start()
    mine_sum = own_part[...] + line(fc2_bias) + mlp[mine_at, :]
    back.wait_recv()
    out[...] = (mine_sum + mlp_in[...].astype(F32)).astype(BF16)

    for copy in copies_a + copies_ay + copies_as + copies_n + copies_s:
        copy.wait_send()
    for up, down in copies_k:
        pl.when(has_next)(up.wait_send)
        pl.when(has_prev)(down.wait_send)
    pl.when(has_next)(seg_up.wait_send)
    pl.when(has_prev)(seg_down.wait_send)
    for copy in [cross, cross_v, give, back, on_right, on_left]:
        copy.wait_send()
    each_core(end_b)
    for k in range(3):
        bx_copy(k).wait_send()
        bxs_copy(k).wait_send()
        mixed_copy(k).wait_send()
    for part in (0, 1):
        for i in range(3):
            first_copy(part, i).wait_send()
        for k in range(4):
            for i in range(2):
                second_copy(part, k, i).wait_send()
                hand_copy(part, k, i).wait_send()


def layer_call(*operands):
    vmem = pl.BlockSpec(memory_space=pltpu.VMEM)
    hbm = pl.BlockSpec(memory_space=pl.ANY)
    edge = pl.BlockSpec((128, WIDTH), lambda i: (8, 0))
    dma = pltpu.SemaphoreType.DMA
    scratch = [
        pltpu.VMEM((TOK, WIDTH), F32),
        pltpu.VMEM((4, TOK, WIDTH), BF16),
        pltpu.VMEM((3, 4, 8, 256), F32),
        pltpu.VMEM((4, 8, 5 * TOK), F32),
        pltpu.VMEM((4, TOK, 128), F32),
        pltpu.VMEM((4, QROWS, WIDTH), BF16),
        pltpu.VMEM((WIDTH, WIDTH), BF16),
        pltpu.VMEM((4, 320, WIDTH), BF16),
        pltpu.VMEM((4, 256, 384), BF16),
        pltpu.VMEM((4, TOK, 384), BF16),
        pltpu.VMEM((3, TOK, 384), BF16),
        pltpu.VMEM((4, 4, TOK, 128), F32),
        pltpu.VMEM((4, 4, TOK, 128), F32),
        pltpu.VMEM((4, 4, TOK, 256), F32),
        pltpu.VMEM((ROW, 512), BF16),
        pltpu.VMEM((3 * ROW, 640), BF16),
        pltpu.VMEM((TOK, WIDTH), F32),
        pltpu.VMEM((2 * WIDTH, WIDTH), BF16),
        pltpu.VMEM((2 * WIDTH, WIDTH), BF16),
        pltpu.VMEM((8, WIDTH), F32),
        pltpu.VMEM((8, WIDTH), F32),
        pltpu.VMEM((3 * HEAD, WIDTH), BF16),
        pltpu.VMEM((HEAD, WIDTH), BF16),
        pltpu.VMEM((2, TOK, WIDTH), BF16),
        pltpu.VMEM((2 * TOK, WIDTH), BF16),
        pltpu.VMEM((2 * TOK, WIDTH), F32),
        pltpu.VMEM((TOK, WIDTH), BF16),
        pltpu.VMEM((TOK, WIDTH), BF16),
        dma((4,)),
    ]
    for shape in ((4,), (3, 3), (3,), (4,), (3,), (4,), (5,), (2, 4), (2,), (2, 3), (2, 4, 4), (6,), (3,), (2,)):
        scratch += [dma(shape), dma(shape)]
    return pl.pallas_call(
        layer_kernel,
        out_shape=jax.ShapeDtypeStruct((TOK, WIDTH), BF16),
        grid=(1,),
        in_specs=[vmem] * 13 + [hbm] * 4 + [edge] * 2,
        out_specs=vmem,
        scratch_shapes=scratch,
        compiler_params=pltpu.CompilerParams(
            collective_id=0, has_side_effects=True, vmem_limit_bytes=60 << 20
        ),
        name="encoder_layer",
    )(*operands)


def per_device(
    patches,
    seg_ids,
    pos_rows,
    pos_cols,
    row_table,
    col_table,
    ln1_gain,
    ln1_bias,
    w_qkv,
    w_out,
    out_bias,
    ln2_gain,
    ln2_bias,
    w_fc1,
    fc1_bias,
    w_fc2,
    fc2_bias,
):
    w_1 = w_fc1.T
    return layer_call(
        patches[0],
        seg_ids,
        pos_rows,
        pos_cols,
        row_table,
        col_table,
        ln1_gain,
        ln1_bias,
        ln2_gain,
        ln2_bias,
        out_bias,
        fc2_bias,
        fc1_bias,
        w_qkv.T,
        w_out,
        w_1,
        w_fc2,
        w_1,
        w_fc2,
    )[None]


def solution(mesh):
    torus = Mesh(mesh.devices.reshape(4, 4, 4, 2, 2), AXES)
    in_specs = (
        P(BATCH, SEQ, None),
        P(BATCH, SEQ),
        P(BATCH, SEQ),
        P(BATCH, SEQ),
        P(),
        P(),
        P(),
        P(),
        P(None, SEQ),
        P(SEQ, None),
        P(),
        P(),
        P(),
        P(None, ("zh", "c")),
        P(("zh", "c")),
        P(("zh", "c"), None),
        P(),
    )
    return jax.shard_map(
        per_device,
        mesh=torus,
        in_specs=in_specs,
        out_specs=P(BATCH, SEQ, None),
        check_vma=False,
    )
```

```python
import math

import jax
import jax.numpy as jnp
from jax import lax
from jax.experimental import pallas as pl
from jax.experimental.pallas import tpu as pltpu
from jax.sharding import Mesh
from jax.sharding import PartitionSpec as P

AXES = ("zl", "x", "y", "zh", "c")
SEQ = ("zl", "x")
BATCH = ("y", "zh", "c")
MESH_ID = pl.DeviceIdType.MESH
TOK = 192
WIDTH = 1152
ROW = 4 * TOK
HEAD = 72
QROWS = 256
F32 = jnp.float32
BF16 = jnp.bfloat16
NT = (((1,), (1,)), ((), ()))


def norm_rows(values, gain, shift):
    center = jnp.mean(values, -1, keepdims=True)
    moved = values - center
    spread = jnp.mean(jnp.square(moved), -1, keepdims=True)
    return moved * lax.rsqrt(spread + 1e-06) * gain + shift


def line(ref):
    return ref[...].astype(F32).reshape(1, WIDTH)


def gelu(u):
    return 0.5 * u * (1.0 + jnp.tanh(math.sqrt(2.0 / math.pi) * (u + 0.044715 * u * u * u)))


def layer_kernel(
    patches,
    seg_in,
    rows_in,
    cols_in,
    rows_tab,
    cols_tab,
    ln1_gain,
    ln1_bias,
    ln2_gain,
    ln2_bias,
    out_bias,
    fc2_bias,
    fc1_bias,
    w_a,
    w_b,
    w_1,
    w_2,
    tail_1,
    tail_2,
    out,
    emb,
    nrm,
    segs,
    seg_keys,
    seg_query,
    wz,
    wp,
    wof,
    pick,
    mixed_out,
    mixed_in,
    top_own,
    sum_own,
    mix_own,
    qs,
    kv,
    own_part,
    f_own,
    f_far,
    bias_own,
    bias_far,
    stage_a,
    stage_b,
    n2,
    hid,
    mlp,
    mlp_out,
    mlp_in,
    loc_sem,
    a_send,
    a_recv,
    ay_send,
    ay_recv,
    as_send,
    as_recv,
    b_send,
    b_recv,
    bs_send,
    bs_recv,
    n_send,
    n_recv,
    s_send,
    s_recv,
    k_send,
    k_recv,
    f_send,
    f_recv,
    f1_send,
    f1_recv,
    f2_send,
    f2_recv,
    bx_send,
    bx_recv,
    r_send,
    r_recv,
    m_send,
    m_recv,
):
    zl, x, y, zh, c = (lax.axis_index(a) for a in AXES)
    z = zh * 4 + zl

    def device(dz=0, dx=0, dy=0, dc=0, mirror=False):
        zz = 7 - z if mirror else lax.rem(z + dz + 8, 8)
        return {
            "zl": lax.rem(zz, 4),
            "x": lax.rem(x + dx + 4, 4),
            "y": lax.rem(y + dy + 4, 4),
            "zh": zz // 4,
            "c": lax.rem(c + dc, 2),
        }

    def remote(src, dst, send, recv, **where):
        return pltpu.make_async_remote_copy(
            src_ref=src,
            dst_ref=dst,
            send_sem=send,
            recv_sem=recv,
            device_id=device(**where),
            device_id_type=MESH_ID,
        )

    def around(v, d):
        return lax.rem(v + d + 4, 4)

    has_prev = zl > 0
    has_next = zl < 3

    barrier = pltpu.get_barrier_semaphore()
    peers = (
        [dict(dz=d) for d in (1, -1, 2, -2)]
        + [dict(dx=d) for d in (1, -1, 2)]
        + [dict(dy=d) for d in (1, -1, 2)]
        + [dict(dc=1), dict(mirror=True)]
    )
    for peer in peers:
        pl.semaphore_signal(barrier, inc=1, device_id=device(**peer), device_id_type=MESH_ID)

    local = [
        pltpu.make_async_copy(w_a, stage_a, loc_sem.at[0]),
        pltpu.make_async_copy(w_b, stage_b, loc_sem.at[1]),
        pltpu.make_async_copy(w_1.at[0:1024], f_own.at[0:1024], loc_sem.at[2]),
        pltpu.make_async_copy(w_2.at[0:1024], f_own.at[1152:2176], loc_sem.at[3]),
    ]
    for copy in local:
        copy.start()

    local[0].wait()
    staged = stage_a[...].astype(F32)
    wz[zl] = jnp.concatenate(
        [
            staged[:HEAD],
            jnp.zeros((8, WIDTH), F32),
            staged[HEAD:],
            jnp.zeros((QROWS - 8 - 3 * HEAD, WIDTH), F32),
        ],
        axis=0,
    ).astype(BF16)
    pl.semaphore_wait(barrier, len(peers))

    def slab(buf, first, rows, send, recv, k, dz):
        ref = buf.at[zl, pl.ds(pl.multiple_of(first, 16), rows)]
        return remote(ref, ref, send.at[k], recv.at[k], dz=dz)

    eighth = (c * 4 + y) * 32
    copies_a = [
        slab(wz, eighth, 32, a_send, a_recv, 0, 1),
        slab(wz, eighth, 32, a_send, a_recv, 1, -1),
        slab(wz, eighth, 16, a_send, a_recv, 2, 2),
        slab(wz, eighth + 16, 16, a_send, a_recv, 3, -2),
    ]
    for copy in copies_a:
        copy.start()

    def wide(ref):
        return jnp.concatenate([ref[...].astype(F32), jnp.zeros((1, 64), F32)], axis=1)

    level = lax.broadcasted_iota(jnp.int32, (128, 256), 0).astype(F32)
    wanted = jnp.where(level < 64.0, wide(rows_in), wide(cols_in) + 64.0)
    hot = jnp.transpose(jnp.where(level == wanted, 1.0, 0.0))[:TOK].astype(BF16)
    tables = jnp.concatenate([rows_tab[...], cols_tab[...]], axis=0)
    embedded = patches[...].astype(F32) + jnp.dot(hot, tables, preferred_element_type=F32)
    emb[...] = embedded
    nrm[x] = norm_rows(embedded, line(ln1_gain), line(ln1_bias)).astype(BF16)
    segs[1, x] = jnp.broadcast_to(wide(seg_in), (8, 256))
    short = fc1_bias.shape[0]
    wide_bias = jnp.concatenate(
        [fc1_bias[...].astype(F32).reshape(1, short), jnp.zeros((1, WIDTH - short), F32)], axis=1
    )
    bias_own[...] = jnp.broadcast_to(wide_bias, (8, WIDTH))

    LOW, HIGH = pl.ds(0, 96), pl.ds(96, 96)
    copies_n = [
        remote(nrm.at[x], nrm.at[x], n_send.at[k], n_recv.at[k], dx=dx)
        for k, dx in enumerate((1, -1))
    ]
    copies_s = [
        remote(segs.at[1, x], segs.at[1, x], s_send.at[k], s_recv.at[k], dx=dx)
        for k, dx in enumerate((1, -1, 2))
    ]
    for copy in copies_n + copies_s:
        copy.start()

    local[1].wait()
    wof[x, pl.ds(pl.multiple_of(zl * 80, 16), 80)] = jnp.concatenate(
        [stage_b[...].astype(F32), jnp.zeros((8, WIDTH), F32)], axis=0
    ).astype(BF16)

    for copy in copies_a:
        copy.wait_recv()
    copies_ay = []
    for k, d in enumerate((-1, 1, 2)):
        for i, dy in enumerate((1, -1, 2)):
            ref = wz.at[around(zl, d), pl.ds(pl.multiple_of(eighth, 16), 32)]
            copies_ay.append(remote(ref, ref, ay_send.at[k, i], ay_recv.at[k, i], dy=dy))
    for copy in copies_ay:
        copy.start()

    def unit(py, px, first, rows):
        at = pl.multiple_of((py * 4 + px) * 144 + first, 16)
        return f_far.at[pl.ds(at, rows)]

    for copy in local[2:]:
        copy.wait()
    rest = w_1.shape[0] - 1024
    mine = pl.ds(pl.multiple_of((y * 4 + x) * 144, 16), 144)
    cross = remote(f_own.at[mine], f_far.at[mine], f_send.at[0], f_recv.at[0], mirror=True)
    cross_v = remote(bias_own, bias_far, f_send.at[1], f_recv.at[1], mirror=True)
    real = lax.broadcasted_iota(jnp.int32, (128, WIDTH), 0) < rest
    f_own[1024:1152, :] = jnp.where(real, tail_1[...], jnp.zeros((128, WIDTH), BF16))
    f_own[2176:2304, :] = jnp.where(real, tail_2[...], jnp.zeros((128, WIDTH), BF16))
    cross.start()
    cross_v.start()

    B_CUTS = ((0, 48), (48, 32))

    def rows_of(owner, core):
        first, rows = B_CUTS[core]
        return pl.ds(pl.multiple_of(owner * 80 + first, 16), rows)

    def b_copies(core):
        ref = wof.at[x, rows_of(zl, core)]
        return [
            remote(ref, ref, b_send.at[k], b_recv.at[k], dz=dz)
            for k, dz in enumerate((1, -1, (2, -2)[core]))
        ]

    def bs_copies(core):
        made = []
        for k, d in enumerate((-1, 1, 2)):
            ref = wof.at[x, rows_of(around(zl, d), core)]
            made.append(remote(ref, ref, bs_send.at[k], bs_recv.at[k], dc=1))
        return made

    def each_core(act):
        for core in (0, 1):

            @pl.when(c == core)
            def _():
                act(core)

    def start_b(core):
        for copy in b_copies(core):
            copy.start()

    def pass_b(core):
        for copy in b_copies(core):
            copy.wait_recv()
        for copy in bs_copies(core):
            copy.start()

    def take_b(core):
        for copy in bs_copies(1 - core):
            copy.wait_recv()

    def end_b(core):
        for copy in b_copies(core) + bs_copies(core):
            copy.wait_send()

    half_o = pl.ds(pl.multiple_of(c * 160, 16), 160)

    def bx_copy(k):
        ref = wof.at[x, half_o]
        return remote(ref, ref, bx_send.at[k], bx_recv.at[k], dx=(1, -1)[k])

    def bx_hand(k):
        at = pl.ds(pl.multiple_of(c * 160 + 80 * k, 16), 80)
        ref = wof.at[around(x, (-1, 1)[k]), at]
        return remote(ref, ref, bx_send.at[2 + k], bx_recv.at[2 + k], dx=(1, -1)[k])

    def bxs_copy(k):
        ref = wof.at[around(x, (-1, 1, 2)[k]), half_o]
        return remote(ref, ref, bx_send.at[4 + k], bx_recv.at[4 + k], dc=1)

    each_core(start_b)

    wp[...] = jnp.zeros_like(wp)
    lane = lax.broadcasted_iota(jnp.int32, (256, 384), 1)
    line_of = lax.broadcasted_iota(jnp.int32, (256, 384), 0)
    for h in range(4):
        feature = lane - 80 * h
        chosen = (line_of - (16 * h + HEAD) == feature) & (feature >= 0) & (feature < HEAD)
        pick[h] = jnp.where(chosen, 1.0, 0.0).astype(BF16)

    @pl.when(jnp.logical_not(has_prev))
    def _():
        kv[0:ROW, :] = jnp.zeros((ROW, 640), BF16)
        segs[0] = jnp.full((4, 8, 256), -1.0, F32)

    @pl.when(jnp.logical_not(has_next))
    def _():
        kv[ROW : 2 * ROW, :] = jnp.zeros((ROW, 640), BF16)
        segs[2] = jnp.full((4, 8, 256), -1.0, F32)

    left, right, far_x = around(x, -1), around(x, 1), around(x, 2)
    copies_n[0].wait_recv()
    on_right = remote(nrm.at[left, LOW], nrm.at[left, LOW], n_send.at[2], n_recv.at[2], dx=1)
    on_right.start()
    copies_n[1].wait_recv()
    on_left = remote(nrm.at[right, HIGH], nrm.at[right, HIGH], n_send.at[3], n_recv.at[3], dx=-1)
    on_left.start()

    def to_sibling(buf, first, rows, send, recv):
        at = pl.ds(pl.multiple_of(first, 16), rows)
        made = []
        for k, d in enumerate((-1, 1, 2)):
            ref = buf.at[around(zl, d), at]
            made.append(remote(ref, ref, send.at[k], recv.at[k], dc=1))
        return made

    copies_as = to_sibling(wz, c * (QROWS // 2), QROWS // 2, as_send, as_recv)
    for copy in copies_ay:
        copy.wait_recv()
    for copy in copies_as:
        copy.start()
    for copy in copies_as:
        copy.wait_recv()
    for h in range(4):
        wp[144 * h : 144 * h + 80, :] = wz[h, 0:80, :]
        wp[512 + 144 * h : 656 + 144 * h, :] = wz[h, 80:224, :]

    copies_k = []

    def project(k, source):
        tokens = nrm[source]
        at = pl.ds(pl.multiple_of(source * TOK, TOK), TOK)
        here = pl.ds(pl.multiple_of(2 * ROW + source * TOK, TOK), TOK)
        as_next = pl.ds(pl.multiple_of(ROW + source * TOK, TOK), TOK)
        kv[here, :] = lax.dot_general(
            tokens, wp[512:1152, :], NT, preferred_element_type=F32
        ).astype(BF16)
        up = remote(kv.at[here], kv.at[at], k_send.at[0, k], k_recv.at[0, k], dz=1)
        down = remote(kv.at[here], kv.at[as_next], k_send.at[1, k], k_recv.at[1, k], dz=-1)
        copies_k.append((up, down))
        pl.when(has_next)(up.start)
        pl.when(has_prev)(down.start)
        qs[at, :] = lax.dot_general(
            tokens, wp[0:512, :], NT, preferred_element_type=F32
        ).astype(BF16)

    PARTS = ((0, 112, 64), (112, 32, 16))
    def held(part, k, db=0):
        d = (0, -1, 1, 2)[k]
        if part == 0:
            return around(y, db), around(x, d)
        return around(y, d), around(x, db)

    def along(part, phase, d):
        return dict(dx=d) if (part == 0) == (phase == 0) else dict(dy=d)

    def first_copy(part, i):
        first, rows, _ = PARTS[part]
        ref = unit(y, x, first, rows)
        d = (1, -1, 2)[i]
        return remote(ref, ref, f1_send.at[part, i], f1_recv.at[part, i], **along(part, 0, d))

    def second_copy(part, k, i):
        first, rows, _ = PARTS[part]
        ref = unit(*held(part, k), first, rows)
        return remote(
            ref, ref, f2_send.at[part, k, i], f2_recv.at[part, k, i], **along(part, 1, (1, -1)[i])
        )

    def hand_copy(part, k, i):
        first, rows, half = PARTS[part]
        cut = ((first, half), (first + half, rows - half))[i]
        d = (1, -1)[i]
        ref = unit(*held(part, k, -d), *cut)
        at = (part, k, 2 + i)
        return remote(ref, ref, f2_send.at[at], f2_recv.at[at], **along(part, 1, d))

    def start_first(part):
        for i in range(3):
            first_copy(part, i).start()

    def start_second(part, k):
        for i in range(2):
            second_copy(part, k, i).start()

    def hand_on(part, k):
        for i in range(2):
            second_copy(part, k, i).wait_recv()
            hand_copy(part, k, i).start()

    project(0, x)
    cross.wait_recv()
    for part in (0, 1):
        start_first(part)
        start_second(part, 0)
    project(1, left)
    project(2, right)

    on_right.wait_recv()
    on_left.wait_recv()
    project(3, far_x)
    each_core(pass_b)
    each_core(take_b)
    for copy in copies_s:
        copy.wait_recv()
    seg_up = remote(segs.at[1], segs.at[0], s_send.at[3], s_recv.at[3], dz=1)
    seg_down = remote(segs.at[1], segs.at[2], s_send.at[4], s_recv.at[4], dz=-1)
    pl.when(has_next)(seg_up.start)
    pl.when(has_prev)(seg_down.start)


    scale = 1.0 / math.sqrt(HEAD)
    seg_keys[0] = jnp.concatenate([segs[1, b][:, :TOK] for b in range(4)] + [segs[1, 0][:, :TOK]], axis=1)
    for j in range(4):
        spread = jnp.concatenate([segs[1, j]] * 16, axis=0)
        seg_query[j] = jnp.transpose(spread)[:TOK]

    def scores_of(j, h, keys):
        at = pl.ds(pl.multiple_of(j * TOK, TOK), TOK)
        return lax.dot_general(
            qs[at, 128 * h : 128 * h + 128],
            kv[keys, 128 * h : 128 * h + 128],
            NT,
            preferred_element_type=F32,
        )

    def attend_own(j):
        same = seg_query[j][:, 0:1] == seg_keys[0][0:1, :ROW]
        own = pl.ds(2 * ROW, ROW)
        for h in range(4):
            scores = jnp.where(same, scores_of(j, h, own), -jnp.inf)
            top = jnp.max(scores, -1, keepdims=True)
            expo = jnp.exp((scores - top) * scale)
            top_own[j, h] = jnp.broadcast_to(top, (TOK, 128))
            sum_own[j, h] = jnp.broadcast_to(jnp.sum(expo, -1, keepdims=True), (TOK, 128))
            mix_own[j, h] = jnp.dot(
                expo.astype(BF16), kv[own, 128 * h : 128 * h + 256], preferred_element_type=F32
            )

    def own_steps(first):
        def step(j, carry):
            attend_own(j)
            return carry

        lax.fori_loop(first, first + 2, step, 0)

    for k in (1, 2, 3):
        for part in (1, 0):
            first_copy(part, k - 1).wait_recv()
            start_second(part, k)
    for k in range(2):
        bx_copy(k).start()
    own_steps(0)
    for part in (1, 0):
        hand_on(part, 0)
    own_steps(2)
    for k in range(2):
        bx_copy(k).wait_recv()
        bx_hand(k).start()
        bxs_copy(k).start()
    for part in (1, 0):
        hand_on(part, 1)

    pl.when(has_prev)(seg_up.wait_recv)
    pl.when(has_next)(seg_down.wait_recv)
    around_segs = [segs[r, b][:, :TOK] for r in (0, 2) for b in range(4)]
    for j in range(4):
        seg_keys[j] = jnp.concatenate(around_segs[j : j + 5], axis=1)
    for up, down in copies_k:
        pl.when(has_prev)(up.wait_recv)
        pl.when(has_next)(down.wait_recv)

    def attend(j):
        window = pl.ds(pl.multiple_of(j * TOK, TOK), 5 * TOK)
        same = seg_query[j][:, 0:1] == seg_keys[j][0:1, :]
        total = None
        for h in range(4):
            scores = jnp.where(same, scores_of(j, h, window), -jnp.inf)
            before = top_own[j, h][:, 0:1]
            top = jnp.maximum(jnp.max(scores, -1, keepdims=True), before)
            expo = jnp.exp((scores - top) * scale)
            kept = jnp.exp((before - top) * scale)
            weight = jnp.sum(expo, -1, keepdims=True) + kept * sum_own[j, h][:, 0:1]
            mixed = jnp.dot(
                expo.astype(BF16), kv[window, 128 * h : 128 * h + 256], preferred_element_type=F32
            )
            mixed = ((mixed + kept * mix_own[j, h]) / weight).astype(BF16)
            term = jnp.dot(mixed, pick[h], preferred_element_type=F32)
            total = term if total is None else total + term
        return total.astype(BF16)

    def mixed_copy(k):
        return remote(
            mixed_out.at[k], mixed_in.at[k], r_send.at[k], r_recv.at[k], dx=(2, 1, -1)[k]
        )

    def attend_step(k, carry):
        d = jnp.where(k == 0, 2, jnp.where(k == 1, 1, jnp.where(k == 2, 3, 0)))
        got = attend(around(x, d))
        mixed_out[k] = got
        for step in range(3):

            @pl.when(k == step)
            def _():
                mixed_copy(step).start()
                if step < 2:
                    for part in (1, 0):
                        hand_on(part, step + 2)
                if step == 1:
                    bx_hand(0).wait_recv()
                    bx_hand(1).wait_recv()
                    bxs_copy(2).start()

        return carry

    lax.fori_loop(0, 4, attend_step, 0)

    def projected(held_in, px):
        return jnp.dot(held_in[:, 0:320], wof[px], preferred_element_type=F32)

    attended = emb[...] + projected(mixed_out[3], x) + line(out_bias)
    for k in range(3):
        bxs_copy(k).wait_recv()
    for k, d in enumerate((2, -1, 1)):
        mixed_copy(k).wait_recv()
        attended = attended + projected(mixed_in[k], around(x, d))
    own_part[...] = attended
    n2[c] = norm_rows(attended, line(ln2_gain), line(ln2_bias)).astype(BF16)
    give = remote(n2.at[c], n2.at[c], m_send.at[0], m_recv.at[0], dc=1)
    give.start()
    give.wait_recv()

    tokens = n2[...].reshape(2 * TOK, WIDTH)

    def hidden_of(weights, biases):
        def step(i, carry):
            at = pl.ds(pl.multiple_of(i * 384, 384), 384)
            inner = lax.dot_general(tokens, weights[at, :], NT, preferred_element_type=F32)
            hid[:, at] = gelu(inner + biases[0:1, at]).astype(BF16)
            return carry

        lax.fori_loop(0, 3, step, 0, unroll=True)

    def project_hidden(weights, first):
        def step(i, carry):
            at = pl.ds(pl.multiple_of(i * 384, 384), 384)
            got = jnp.dot(hid[...], weights[WIDTH : 2 * WIDTH, at], preferred_element_type=F32)
            mlp[:, at] = got if first else mlp[:, at] + got
            return carry

        lax.fori_loop(0, 3, step, 0, unroll=True)

    hidden_of(f_own, bias_own)
    project_hidden(f_own, True)
    for part in (0, 1):
        for k in range(4):
            for i in range(2):
                hand_copy(part, k, i).wait_recv()
    cross_v.wait_recv()
    hidden_of(f_far, bias_far)
    project_hidden(f_far, False)

    mine_at = pl.ds(pl.multiple_of(c * TOK, TOK), TOK)
    other_at = pl.ds(pl.multiple_of((1 - c) * TOK, TOK), TOK)
    mlp_out[...] = mlp[other_at, :].astype(BF16)
    back = remote(mlp_out, mlp_in, m_send.at[1], m_recv.at[1], dc=1)
    back.start()
    mine_sum = own_part[...] + line(fc2_bias) + mlp[mine_at, :]
    back.wait_recv()
    out[...] = (mine_sum + mlp_in[...].astype(F32)).astype(BF16)

    for copy in copies_a + copies_ay + copies_as + copies_n + copies_s:
        copy.wait_send()
    for up, down in copies_k:
        pl.when(has_next)(up.wait_send)
        pl.when(has_prev)(down.wait_send)
    pl.when(has_next)(seg_up.wait_send)
    pl.when(has_prev)(seg_down.wait_send)
    for copy in [cross, cross_v, give, back, on_right, on_left]:
        copy.wait_send()
    each_core(end_b)
    for k in range(2):
        bx_copy(k).wait_send()
        bx_hand(k).wait_send()
    for k in range(3):
        bxs_copy(k).wait_send()
        mixed_copy(k).wait_send()
    for part in (0, 1):
        for i in range(3):
            first_copy(part, i).wait_send()
        for k in range(4):
            for i in range(2):
                second_copy(part, k, i).wait_send()
                hand_copy(part, k, i).wait_send()


def layer_call(*operands):
    vmem = pl.BlockSpec(memory_space=pltpu.VMEM)
    hbm = pl.BlockSpec(memory_space=pl.ANY)
    edge = pl.BlockSpec((128, WIDTH), lambda i: (8, 0))
    dma = pltpu.SemaphoreType.DMA
    scratch = [
        pltpu.VMEM((TOK, WIDTH), F32),
        pltpu.VMEM((4, TOK, WIDTH), BF16),
        pltpu.VMEM((3, 4, 8, 256), F32),
        pltpu.VMEM((4, 8, 5 * TOK), F32),
        pltpu.VMEM((4, TOK, 128), F32),
        pltpu.VMEM((4, QROWS, WIDTH), BF16),
        pltpu.VMEM((WIDTH, WIDTH), BF16),
        pltpu.VMEM((4, 320, WIDTH), BF16),
        pltpu.VMEM((4, 256, 384), BF16),
        pltpu.VMEM((4, TOK, 384), BF16),
        pltpu.VMEM((3, TOK, 384), BF16),
        pltpu.VMEM((4, 4, TOK, 128), F32),
        pltpu.VMEM((4, 4, TOK, 128), F32),
        pltpu.VMEM((4, 4, TOK, 256), F32),
        pltpu.VMEM((ROW, 512), BF16),
        pltpu.VMEM((3 * ROW, 640), BF16),
        pltpu.VMEM((TOK, WIDTH), F32),
        pltpu.VMEM((2 * WIDTH, WIDTH), BF16),
        pltpu.VMEM((2 * WIDTH, WIDTH), BF16),
        pltpu.VMEM((8, WIDTH), F32),
        pltpu.VMEM((8, WIDTH), F32),
        pltpu.VMEM((3 * HEAD, WIDTH), BF16),
        pltpu.VMEM((HEAD, WIDTH), BF16),
        pltpu.VMEM((2, TOK, WIDTH), BF16),
        pltpu.VMEM((2 * TOK, WIDTH), BF16),
        pltpu.VMEM((2 * TOK, WIDTH), F32),
        pltpu.VMEM((TOK, WIDTH), BF16),
        pltpu.VMEM((TOK, WIDTH), BF16),
        dma((4,)),
    ]
    for shape in ((4,), (3, 3), (3,), (4,), (3,), (4,), (5,), (2, 4), (2,), (2, 3), (2, 4, 4), (7,), (3,), (2,)):
        scratch += [dma(shape), dma(shape)]
    return pl.pallas_call(
        layer_kernel,
        out_shape=jax.ShapeDtypeStruct((TOK, WIDTH), BF16),
        grid=(1,),
        in_specs=[vmem] * 13 + [hbm] * 4 + [edge] * 2,
        out_specs=vmem,
        scratch_shapes=scratch,
        compiler_params=pltpu.CompilerParams(
            collective_id=0, has_side_effects=True, vmem_limit_bytes=60 << 20
        ),
        name="encoder_layer",
    )(*operands)


def per_device(
    patches,
    seg_ids,
    pos_rows,
    pos_cols,
    row_table,
    col_table,
    ln1_gain,
    ln1_bias,
    w_qkv,
    w_out,
    out_bias,
    ln2_gain,
    ln2_bias,
    w_fc1,
    fc1_bias,
    w_fc2,
    fc2_bias,
):
    w_1 = w_fc1.T
    return layer_call(
        patches[0],
        seg_ids,
        pos_rows,
        pos_cols,
        row_table,
        col_table,
        ln1_gain,
        ln1_bias,
        ln2_gain,
        ln2_bias,
        out_bias,
        fc2_bias,
        fc1_bias,
        w_qkv.T,
        w_out,
        w_1,
        w_fc2,
        w_1,
        w_fc2,
    )[None]


def solution(mesh):
    torus = Mesh(mesh.devices.reshape(4, 4, 4, 2, 2), AXES)
    in_specs = (
        P(BATCH, SEQ, None),
        P(BATCH, SEQ),
        P(BATCH, SEQ),
        P(BATCH, SEQ),
        P(),
        P(),
        P(),
        P(),
        P(None, SEQ),
        P(SEQ, None),
        P(),
        P(),
        P(),
        P(None, ("zh", "c")),
        P(("zh", "c")),
        P(("zh", "c"), None),
        P(),
    )
    return jax.shard_map(
        per_device,
        mesh=torus,
        in_specs=in_specs,
        out_specs=P(BATCH, SEQ, None),
        check_vma=False,
    )
```

```python
import math

import jax
import jax.numpy as jnp
from jax import lax
from jax.experimental import pallas as pl
from jax.experimental.pallas import tpu as pltpu
from jax.sharding import Mesh
from jax.sharding import PartitionSpec as P

AXES = ("zl", "x", "y", "zh", "c")
SEQ = ("zl", "x")
BATCH = ("y", "zh", "c")
MESH_ID = pl.DeviceIdType.MESH
TOK = 192
WIDTH = 1152
ROW = 4 * TOK
HEAD = 72
QROWS = 256
F32 = jnp.float32
BF16 = jnp.bfloat16
NT = (((1,), (1,)), ((), ()))


def norm_rows(values, gain, shift):
    center = jnp.mean(values, -1, keepdims=True)
    moved = values - center
    spread = jnp.mean(jnp.square(moved), -1, keepdims=True)
    return moved * lax.rsqrt(spread + 1e-06) * gain + shift


def line(ref):
    return ref[...].astype(F32).reshape(1, WIDTH)


def gelu(u):
    return 0.5 * u * (1.0 + jnp.tanh(math.sqrt(2.0 / math.pi) * (u + 0.044715 * u * u * u)))


def layer_kernel(
    patches,
    seg_in,
    rows_in,
    cols_in,
    rows_tab,
    cols_tab,
    ln1_gain,
    ln1_bias,
    ln2_gain,
    ln2_bias,
    out_bias,
    fc2_bias,
    fc1_bias,
    w_a,
    w_b,
    w_1,
    w_2,
    tail_1,
    tail_2,
    out,
    emb,
    nrm,
    segs,
    seg_keys,
    seg_query,
    wz,
    wp,
    wof,
    pick,
    mixed_out,
    mixed_in,
    top_own,
    sum_own,
    mix_own,
    qs,
    kv,
    own_part,
    f_own,
    f_far,
    bias_own,
    bias_far,
    stage_a,
    stage_b,
    n2,
    hid,
    mlp,
    mlp_out,
    mlp_in,
    loc_sem,
    a_send,
    a_recv,
    ay_send,
    ay_recv,
    as_send,
    as_recv,
    b_send,
    b_recv,
    bs_send,
    bs_recv,
    n_send,
    n_recv,
    s_send,
    s_recv,
    k_send,
    k_recv,
    f_send,
    f_recv,
    f1_send,
    f1_recv,
    f2_send,
    f2_recv,
    bx_send,
    bx_recv,
    r_send,
    r_recv,
    m_send,
    m_recv,
):
    zl, x, y, zh, c = (lax.axis_index(a) for a in AXES)
    z = zh * 4 + zl

    def device(dz=0, dx=0, dy=0, dc=0, mirror=False):
        zz = 7 - z if mirror else lax.rem(z + dz + 8, 8)
        return {
            "zl": lax.rem(zz, 4),
            "x": lax.rem(x + dx + 4, 4),
            "y": lax.rem(y + dy + 4, 4),
            "zh": zz // 4,
            "c": lax.rem(c + dc, 2),
        }

    def remote(src, dst, send, recv, **where):
        return pltpu.make_async_remote_copy(
            src_ref=src,
            dst_ref=dst,
            send_sem=send,
            recv_sem=recv,
            device_id=device(**where),
            device_id_type=MESH_ID,
        )

    def around(v, d):
        return lax.rem(v + d + 4, 4)

    has_prev = zl > 0
    has_next = zl < 3

    barrier = pltpu.get_barrier_semaphore()
    peers = (
        [dict(dz=d) for d in (1, -1, 2, -2)]
        + [dict(dx=d) for d in (1, -1, 2)]
        + [dict(dy=d) for d in (1, -1, 2)]
        + [dict(dc=1), dict(mirror=True)]
    )
    for peer in peers:
        pl.semaphore_signal(barrier, inc=1, device_id=device(**peer), device_id_type=MESH_ID)

    local = [
        pltpu.make_async_copy(w_a, stage_a, loc_sem.at[0]),
        pltpu.make_async_copy(w_b, stage_b, loc_sem.at[1]),
        pltpu.make_async_copy(w_1.at[0:1024], f_own.at[0:1024], loc_sem.at[2]),
        pltpu.make_async_copy(w_2.at[0:1024], f_own.at[1152:2176], loc_sem.at[3]),
    ]
    for copy in local:
        copy.start()

    local[0].wait()
    staged = stage_a[...].astype(F32)
    wz[zl] = jnp.concatenate(
        [
            staged[:HEAD],
            jnp.zeros((8, WIDTH), F32),
            staged[HEAD:],
            jnp.zeros((QROWS - 8 - 3 * HEAD, WIDTH), F32),
        ],
        axis=0,
    ).astype(BF16)
    pl.semaphore_wait(barrier, len(peers))

    def slab(buf, first, rows, send, recv, k, dz):
        ref = buf.at[zl, pl.ds(pl.multiple_of(first, 16), rows)]
        return remote(ref, ref, send.at[k], recv.at[k], dz=dz)

    eighth = (c * 4 + y) * 32
    copies_a = [
        slab(wz, eighth, 32, a_send, a_recv, 0, 1),
        slab(wz, eighth, 32, a_send, a_recv, 1, -1),
        slab(wz, eighth, 16, a_send, a_recv, 2, 2),
        slab(wz, eighth + 16, 16, a_send, a_recv, 3, -2),
    ]
    for copy in copies_a:
        copy.start()

    def wide(ref):
        return jnp.concatenate([ref[...].astype(F32), jnp.zeros((1, 64), F32)], axis=1)

    level = lax.broadcasted_iota(jnp.int32, (128, 256), 0).astype(F32)
    wanted = jnp.where(level < 64.0, wide(rows_in), wide(cols_in) + 64.0)
    hot = jnp.transpose(jnp.where(level == wanted, 1.0, 0.0))[:TOK].astype(BF16)
    tables = jnp.concatenate([rows_tab[...], cols_tab[...]], axis=0)
    embedded = patches[...].astype(F32) + jnp.dot(hot, tables, preferred_element_type=F32)
    emb[...] = embedded
    nrm[x] = norm_rows(embedded, line(ln1_gain), line(ln1_bias)).astype(BF16)
    segs[1, x] = jnp.broadcast_to(wide(seg_in), (8, 256))
    short = fc1_bias.shape[0]
    wide_bias = jnp.concatenate(
        [fc1_bias[...].astype(F32).reshape(1, short), jnp.zeros((1, WIDTH - short), F32)], axis=1
    )
    bias_own[...] = jnp.broadcast_to(wide_bias, (8, WIDTH))

    LOW, HIGH = pl.ds(0, 96), pl.ds(96, 96)
    copies_n = [
        remote(nrm.at[x], nrm.at[x], n_send.at[k], n_recv.at[k], dx=dx)
        for k, dx in enumerate((1, -1))
    ]
    copies_s = [
        remote(segs.at[1, x], segs.at[1, x], s_send.at[k], s_recv.at[k], dx=dx)
        for k, dx in enumerate((1, -1, 2))
    ]
    for copy in copies_n + copies_s:
        copy.start()

    local[1].wait()
    wof[x, pl.ds(pl.multiple_of(zl * 80, 16), 80)] = jnp.concatenate(
        [stage_b[...].astype(F32), jnp.zeros((8, WIDTH), F32)], axis=0
    ).astype(BF16)

    for copy in copies_a:
        copy.wait_recv()
    copies_ay = []
    for k, d in enumerate((-1, 1, 2)):
        for i, dy in enumerate((1, -1, 2)):
            ref = wz.at[around(zl, d), pl.ds(pl.multiple_of(eighth, 16), 32)]
            copies_ay.append(remote(ref, ref, ay_send.at[k, i], ay_recv.at[k, i], dy=dy))
    for copy in copies_ay:
        copy.start()

    def unit(py, px, first, rows):
        at = pl.multiple_of((py * 4 + px) * 144 + first, 16)
        return f_far.at[pl.ds(at, rows)]

    for copy in local[2:]:
        copy.wait()
    rest = w_1.shape[0] - 1024
    mine = pl.ds(pl.multiple_of((y * 4 + x) * 144, 16), 144)
    cross = remote(f_own.at[mine], f_far.at[mine], f_send.at[0], f_recv.at[0], mirror=True)
    cross_v = remote(bias_own, bias_far, f_send.at[1], f_recv.at[1], mirror=True)
    real = lax.broadcasted_iota(jnp.int32, (128, WIDTH), 0) < rest
    f_own[1024:1152, :] = jnp.where(real, tail_1[...], jnp.zeros((128, WIDTH), BF16))
    f_own[2176:2304, :] = jnp.where(real, tail_2[...], jnp.zeros((128, WIDTH), BF16))
    cross.start()
    cross_v.start()

    B_CUTS = ((0, 48), (48, 32))

    def rows_of(owner, core):
        first, rows = B_CUTS[core]
        return pl.ds(pl.multiple_of(owner * 80 + first, 16), rows)

    def b_copies(core):
        ref = wof.at[x, rows_of(zl, core)]
        return [
            remote(ref, ref, b_send.at[k], b_recv.at[k], dz=dz)
            for k, dz in enumerate((1, -1, (2, -2)[core]))
        ]

    def bs_copies(core):
        made = []
        for k, d in enumerate((-1, 1, 2)):
            ref = wof.at[x, rows_of(around(zl, d), core)]
            made.append(remote(ref, ref, bs_send.at[k], bs_recv.at[k], dc=1))
        return made

    def each_core(act):
        for core in (0, 1):

            @pl.when(c == core)
            def _():
                act(core)

    def start_b(core):
        for copy in b_copies(core):
            copy.start()

    def pass_b(core):
        for copy in b_copies(core):
            copy.wait_recv()
        for copy in bs_copies(core):
            copy.start()

    def take_b(core):
        for copy in bs_copies(1 - core):
            copy.wait_recv()

    def end_b(core):
        for copy in b_copies(core) + bs_copies(core):
            copy.wait_send()

    half_o = pl.ds(pl.multiple_of(c * 160, 16), 160)

    def bx_copy(k):
        ref = wof.at[x, half_o]
        return remote(ref, ref, bx_send.at[k], bx_recv.at[k], dx=(1, -1)[k])

    def bx_hand(k):
        at = pl.ds(pl.multiple_of(c * 160 + 80 * k, 16), 80)
        ref = wof.at[around(x, (-1, 1)[k]), at]
        return remote(ref, ref, bx_send.at[2 + k], bx_recv.at[2 + k], dx=(1, -1)[k])

    def bxs_copy(k):
        ref = wof.at[around(x, (-1, 1, 2)[k]), half_o]
        return remote(ref, ref, bx_send.at[4 + k], bx_recv.at[4 + k], dc=1)

    each_core(start_b)

    wp[...] = jnp.zeros_like(wp)
    lane = lax.broadcasted_iota(jnp.int32, (256, 384), 1)
    line_of = lax.broadcasted_iota(jnp.int32, (256, 384), 0)
    for h in range(4):
        feature = lane - 80 * h
        chosen = (line_of - (16 * h + HEAD) == feature) & (feature >= 0) & (feature < HEAD)
        pick[h] = jnp.where(chosen, 1.0, 0.0).astype(BF16)

    @pl.when(jnp.logical_not(has_prev))
    def _():
        kv[0:ROW, :] = jnp.zeros((ROW, 640), BF16)
        segs[0] = jnp.full((4, 8, 256), -1.0, F32)

    @pl.when(jnp.logical_not(has_next))
    def _():
        kv[ROW : 2 * ROW, :] = jnp.zeros((ROW, 640), BF16)
        segs[2] = jnp.full((4, 8, 256), -1.0, F32)

    left, right, far_x = around(x, -1), around(x, 1), around(x, 2)
    copies_n[0].wait_recv()
    on_right = remote(nrm.at[left, LOW], nrm.at[left, LOW], n_send.at[2], n_recv.at[2], dx=1)
    on_right.start()
    copies_n[1].wait_recv()
    on_left = remote(nrm.at[right, HIGH], nrm.at[right, HIGH], n_send.at[3], n_recv.at[3], dx=-1)
    on_left.start()

    def to_sibling(buf, first, rows, send, recv):
        at = pl.ds(pl.multiple_of(first, 16), rows)
        made = []
        for k, d in enumerate((-1, 1, 2)):
            ref = buf.at[around(zl, d), at]
            made.append(remote(ref, ref, send.at[k], recv.at[k], dc=1))
        return made

    copies_as = to_sibling(wz, c * (QROWS // 2), QROWS // 2, as_send, as_recv)
    for copy in copies_ay:
        copy.wait_recv()
    for copy in copies_as:
        copy.start()
    for copy in copies_as:
        copy.wait_recv()
    for h in range(4):
        wp[144 * h : 144 * h + 80, :] = wz[h, 0:80, :]
        wp[512 + 144 * h : 656 + 144 * h, :] = wz[h, 80:224, :]

    copies_k = []

    def project(k, source):
        tokens = nrm[source]
        at = pl.ds(pl.multiple_of(source * TOK, TOK), TOK)
        here = pl.ds(pl.multiple_of(2 * ROW + source * TOK, TOK), TOK)
        as_next = pl.ds(pl.multiple_of(ROW + source * TOK, TOK), TOK)
        kv[here, :] = lax.dot_general(
            tokens, wp[512:1152, :], NT, preferred_element_type=F32
        ).astype(BF16)
        up = remote(kv.at[here], kv.at[at], k_send.at[0, k], k_recv.at[0, k], dz=1)
        down = remote(kv.at[here], kv.at[as_next], k_send.at[1, k], k_recv.at[1, k], dz=-1)
        copies_k.append((up, down))
        pl.when(has_next)(up.start)
        pl.when(has_prev)(down.start)
        qs[at, :] = lax.dot_general(
            tokens, wp[0:512, :], NT, preferred_element_type=F32
        ).astype(BF16)

    PARTS = ((0, 112, 64), (112, 32, 16))
    def held(part, k, db=0):
        d = (0, -1, 1, 2)[k]
        if part == 0:
            return around(y, db), around(x, d)
        return around(y, d), around(x, db)

    def along(part, phase, d):
        return dict(dx=d) if (part == 0) == (phase == 0) else dict(dy=d)

    def first_copy(part, i):
        first, rows, _ = PARTS[part]
        ref = unit(y, x, first, rows)
        d = (1, -1)[i]
        return remote(ref, ref, f1_send.at[part, i], f1_recv.at[part, i], **along(part, 0, d))

    def first_hand(part, i):
        first, rows, half = PARTS[part]
        cut = ((first, half), (first + half, rows - half))[i]
        ref = unit(*held(part, 1 + i), *cut)
        at = (part, 2 + i)
        return remote(ref, ref, f1_send.at[at], f1_recv.at[at], **along(part, 0, (1, -1)[i]))

    def second_copy(part, k, i):
        first, rows, _ = PARTS[part]
        ref = unit(*held(part, k), first, rows)
        return remote(
            ref, ref, f2_send.at[part, k, i], f2_recv.at[part, k, i], **along(part, 1, (1, -1)[i])
        )

    def hand_copy(part, k, i):
        first, rows, half = PARTS[part]
        cut = ((first, half), (first + half, rows - half))[i]
        d = (1, -1)[i]
        ref = unit(*held(part, k, -d), *cut)
        at = (part, k, 2 + i)
        return remote(ref, ref, f2_send.at[at], f2_recv.at[at], **along(part, 1, d))

    def start_first(part):
        for i in range(2):
            first_copy(part, i).start()

    def start_second(part, k):
        for i in range(2):
            second_copy(part, k, i).start()

    def hand_on(part, k):
        for i in range(2):
            second_copy(part, k, i).wait_recv()
            hand_copy(part, k, i).start()

    project(0, x)
    cross.wait_recv()
    for part in (0, 1):
        start_first(part)
        start_second(part, 0)
    project(1, left)
    project(2, right)

    on_right.wait_recv()
    on_left.wait_recv()
    project(3, far_x)
    each_core(pass_b)
    each_core(take_b)
    for copy in copies_s:
        copy.wait_recv()
    seg_up = remote(segs.at[1], segs.at[0], s_send.at[3], s_recv.at[3], dz=1)
    seg_down = remote(segs.at[1], segs.at[2], s_send.at[4], s_recv.at[4], dz=-1)
    pl.when(has_next)(seg_up.start)
    pl.when(has_prev)(seg_down.start)


    scale = 1.0 / math.sqrt(HEAD)
    seg_keys[0] = jnp.concatenate([segs[1, b][:, :TOK] for b in range(4)] + [segs[1, 0][:, :TOK]], axis=1)
    for j in range(4):
        spread = jnp.concatenate([segs[1, j]] * 16, axis=0)
        seg_query[j] = jnp.transpose(spread)[:TOK]

    def scores_of(j, h, keys):
        at = pl.ds(pl.multiple_of(j * TOK, TOK), TOK)
        return lax.dot_general(
            qs[at, 128 * h : 128 * h + 128],
            kv[keys, 128 * h : 128 * h + 128],
            NT,
            preferred_element_type=F32,
        )

    def attend_own(j):
        same = seg_query[j][:, 0:1] == seg_keys[0][0:1, :ROW]
        own = pl.ds(2 * ROW, ROW)
        for h in range(4):
            scores = jnp.where(same, scores_of(j, h, own), -jnp.inf)
            top = jnp.max(scores, -1, keepdims=True)
            expo = jnp.exp((scores - top) * scale)
            top_own[j, h] = jnp.broadcast_to(top, (TOK, 128))
            sum_own[j, h] = jnp.broadcast_to(jnp.sum(expo, -1, keepdims=True), (TOK, 128))
            mix_own[j, h] = jnp.dot(
                expo.astype(BF16), kv[own, 128 * h : 128 * h + 256], preferred_element_type=F32
            )

    def own_steps(first):
        def step(j, carry):
            attend_own(j)
            return carry

        lax.fori_loop(first, first + 2, step, 0)

    for k in (1, 2, 3):
        for part in (1, 0):
            if k < 3:
                first_copy(part, k - 1).wait_recv()
                first_hand(part, k - 1).start()
            else:
                first_hand(part, 0).wait_recv()
                first_hand(part, 1).wait_recv()
            start_second(part, k)
    for k in range(2):
        bx_copy(k).start()
    own_steps(0)
    for part in (1, 0):
        hand_on(part, 0)
    own_steps(2)
    for k in range(2):
        bx_copy(k).wait_recv()
        bx_hand(k).start()
        bxs_copy(k).start()
    for part in (1, 0):
        hand_on(part, 1)

    pl.when(has_prev)(seg_up.wait_recv)
    pl.when(has_next)(seg_down.wait_recv)
    around_segs = [segs[r, b][:, :TOK] for r in (0, 2) for b in range(4)]
    for j in range(4):
        seg_keys[j] = jnp.concatenate(around_segs[j : j + 5], axis=1)
    for up, down in copies_k:
        pl.when(has_prev)(up.wait_recv)
        pl.when(has_next)(down.wait_recv)

    def attend(j):
        window = pl.ds(pl.multiple_of(j * TOK, TOK), 5 * TOK)
        same = seg_query[j][:, 0:1] == seg_keys[j][0:1, :]
        total = None
        for h in range(4):
            scores = jnp.where(same, scores_of(j, h, window), -jnp.inf)
            before = top_own[j, h][:, 0:1]
            top = jnp.maximum(jnp.max(scores, -1, keepdims=True), before)
            expo = jnp.exp((scores - top) * scale)
            kept = jnp.exp((before - top) * scale)
            weight = jnp.sum(expo, -1, keepdims=True) + kept * sum_own[j, h][:, 0:1]
            mixed = jnp.dot(
                expo.astype(BF16), kv[window, 128 * h : 128 * h + 256], preferred_element_type=F32
            )
            mixed = ((mixed + kept * mix_own[j, h]) / weight).astype(BF16)
            term = jnp.dot(mixed, pick[h], preferred_element_type=F32)
            total = term if total is None else total + term
        return total.astype(BF16)

    def mixed_copy(k):
        return remote(
            mixed_out.at[k], mixed_in.at[k], r_send.at[k], r_recv.at[k], dx=(2, 1, -1)[k]
        )

    def attend_step(k, carry):
        d = jnp.where(k == 0, 2, jnp.where(k == 1, 1, jnp.where(k == 2, 3, 0)))
        got = attend(around(x, d))
        mixed_out[k] = got
        for step in range(3):

            @pl.when(k == step)
            def _():
                mixed_copy(step).start()
                if step < 2:
                    for part in (1, 0):
                        hand_on(part, step + 2)
                if step == 1:
                    bx_hand(0).wait_recv()
                    bx_hand(1).wait_recv()
                    bxs_copy(2).start()

        return carry

    lax.fori_loop(0, 4, attend_step, 0)

    def projected(held_in, px):
        return jnp.dot(held_in[:, 0:320], wof[px], preferred_element_type=F32)

    attended = emb[...] + projected(mixed_out[3], x) + line(out_bias)
    for k in range(3):
        bxs_copy(k).wait_recv()
    for k, d in enumerate((2, -1, 1)):
        mixed_copy(k).wait_recv()
        attended = attended + projected(mixed_in[k], around(x, d))
    own_part[...] = attended
    n2[c] = norm_rows(attended, line(ln2_gain), line(ln2_bias)).astype(BF16)
    give = remote(n2.at[c], n2.at[c], m_send.at[0], m_recv.at[0], dc=1)
    give.start()
    give.wait_recv()

    tokens = n2[...].reshape(2 * TOK, WIDTH)

    def hidden_of(weights, biases):
        def step(i, carry):
            at = pl.ds(pl.multiple_of(i * 384, 384), 384)
            inner = lax.dot_general(tokens, weights[at, :], NT, preferred_element_type=F32)
            hid[:, at] = gelu(inner + biases[0:1, at]).astype(BF16)
            return carry

        lax.fori_loop(0, 3, step, 0, unroll=True)

    def project_hidden(weights, first):
        def step(i, carry):
            at = pl.ds(pl.multiple_of(i * 384, 384), 384)
            got = jnp.dot(hid[...], weights[WIDTH : 2 * WIDTH, at], preferred_element_type=F32)
            mlp[:, at] = got if first else mlp[:, at] + got
            return carry

        lax.fori_loop(0, 3, step, 0, unroll=True)

    hidden_of(f_own, bias_own)
    project_hidden(f_own, True)
    for part in (0, 1):
        for k in range(4):
            for i in range(2):
                hand_copy(part, k, i).wait_recv()
    cross_v.wait_recv()
    hidden_of(f_far, bias_far)
    project_hidden(f_far, False)

    mine_at = pl.ds(pl.multiple_of(c * TOK, TOK), TOK)
    other_at = pl.ds(pl.multiple_of((1 - c) * TOK, TOK), TOK)
    mlp_out[...] = mlp[other_at, :].astype(BF16)
    back = remote(mlp_out, mlp_in, m_send.at[1], m_recv.at[1], dc=1)
    back.start()
    mine_sum = own_part[...] + line(fc2_bias) + mlp[mine_at, :]
    back.wait_recv()
    out[...] = (mine_sum + mlp_in[...].astype(F32)).astype(BF16)

    for copy in copies_a + copies_ay + copies_as + copies_n + copies_s:
        copy.wait_send()
    for up, down in copies_k:
        pl.when(has_next)(up.wait_send)
        pl.when(has_prev)(down.wait_send)
    pl.when(has_next)(seg_up.wait_send)
    pl.when(has_prev)(seg_down.wait_send)
    for copy in [cross, cross_v, give, back, on_right, on_left]:
        copy.wait_send()
    each_core(end_b)
    for k in range(2):
        bx_copy(k).wait_send()
        bx_hand(k).wait_send()
    for k in range(3):
        bxs_copy(k).wait_send()
        mixed_copy(k).wait_send()
    for part in (0, 1):
        for i in range(2):
            first_copy(part, i).wait_send()
            first_hand(part, i).wait_send()
        for k in range(4):
            for i in range(2):
                second_copy(part, k, i).wait_send()
                hand_copy(part, k, i).wait_send()


def layer_call(*operands):
    vmem = pl.BlockSpec(memory_space=pltpu.VMEM)
    hbm = pl.BlockSpec(memory_space=pl.ANY)
    edge = pl.BlockSpec((128, WIDTH), lambda i: (8, 0))
    dma = pltpu.SemaphoreType.DMA
    scratch = [
        pltpu.VMEM((TOK, WIDTH), F32),
        pltpu.VMEM((4, TOK, WIDTH), BF16),
        pltpu.VMEM((3, 4, 8, 256), F32),
        pltpu.VMEM((4, 8, 5 * TOK), F32),
        pltpu.VMEM((4, TOK, 128), F32),
        pltpu.VMEM((4, QROWS, WIDTH), BF16),
        pltpu.VMEM((WIDTH, WIDTH), BF16),
        pltpu.VMEM((4, 320, WIDTH), BF16),
        pltpu.VMEM((4, 256, 384), BF16),
        pltpu.VMEM((4, TOK, 384), BF16),
        pltpu.VMEM((3, TOK, 384), BF16),
        pltpu.VMEM((4, 4, TOK, 128), F32),
        pltpu.VMEM((4, 4, TOK, 128), F32),
        pltpu.VMEM((4, 4, TOK, 256), F32),
        pltpu.VMEM((ROW, 512), BF16),
        pltpu.VMEM((3 * ROW, 640), BF16),
        pltpu.VMEM((TOK, WIDTH), F32),
        pltpu.VMEM((2 * WIDTH, WIDTH), BF16),
        pltpu.VMEM((2 * WIDTH, WIDTH), BF16),
        pltpu.VMEM((8, WIDTH), F32),
        pltpu.VMEM((8, WIDTH), F32),
        pltpu.VMEM((3 * HEAD, WIDTH), BF16),
        pltpu.VMEM((HEAD, WIDTH), BF16),
        pltpu.VMEM((2, TOK, WIDTH), BF16),
        pltpu.VMEM((2 * TOK, WIDTH), BF16),
        pltpu.VMEM((2 * TOK, WIDTH), F32),
        pltpu.VMEM((TOK, WIDTH), BF16),
        pltpu.VMEM((TOK, WIDTH), BF16),
        dma((4,)),
    ]
    for shape in ((4,), (3, 3), (3,), (4,), (3,), (4,), (5,), (2, 4), (2,), (2, 4), (2, 4, 4), (7,), (3,), (2,)):
        scratch += [dma(shape), dma(shape)]
    return pl.pallas_call(
        layer_kernel,
        out_shape=jax.ShapeDtypeStruct((TOK, WIDTH), BF16),
        grid=(1,),
        in_specs=[vmem] * 13 + [hbm] * 4 + [edge] * 2,
        out_specs=vmem,
        scratch_shapes=scratch,
        compiler_params=pltpu.CompilerParams(
            collective_id=0, has_side_effects=True, vmem_limit_bytes=60 << 20
        ),
        name="encoder_layer",
    )(*operands)


def per_device(
    patches,
    seg_ids,
    pos_rows,
    pos_cols,
    row_table,
    col_table,
    ln1_gain,
    ln1_bias,
    w_qkv,
    w_out,
    out_bias,
    ln2_gain,
    ln2_bias,
    w_fc1,
    fc1_bias,
    w_fc2,
    fc2_bias,
):
    w_1 = w_fc1.T
    return layer_call(
        patches[0],
        seg_ids,
        pos_rows,
        pos_cols,
        row_table,
        col_table,
        ln1_gain,
        ln1_bias,
        ln2_gain,
        ln2_bias,
        out_bias,
        fc2_bias,
        fc1_bias,
        w_qkv.T,
        w_out,
        w_1,
        w_fc2,
        w_1,
        w_fc2,
    )[None]


def solution(mesh):
    torus = Mesh(mesh.devices.reshape(4, 4, 4, 2, 2), AXES)
    in_specs = (
        P(BATCH, SEQ, None),
        P(BATCH, SEQ),
        P(BATCH, SEQ),
        P(BATCH, SEQ),
        P(),
        P(),
        P(),
        P(),
        P(None, SEQ),
        P(SEQ, None),
        P(),
        P(),
        P(),
        P(None, ("zh", "c")),
        P(("zh", "c")),
        P(("zh", "c"), None),
        P(),
    )
    return jax.shard_map(
        per_device,
        mesh=torus,
        in_specs=in_specs,
        out_specs=P(BATCH, SEQ, None),
        check_vma=False,
    )
```
